512 devices in a mesh: seq: 128 (over z_lo, x, y, core), head: 4 (over z_hi).
Axes of the slice: x: 4, y: 8, z: 8 (z_hi: 4, z_lo: 2; z = z_hi * 2 + z_lo), core: 2. Of those that a mesh axis runs over, the one named last changes fastest.
Arguments:
- queries: bfloat16 [65536, 1024], P('seq', 'head'), may hold values from -6 to 6
- keys: bfloat16 [65536, 1024], P('seq', 'head'), may hold values from -6 to 6
- values: bfloat16 [65536, 1024], P('seq', 'head'), may hold values from -6 to 6
- block_keep: int32 [256], replicated, may hold values 0 or 1
- w_out: bfloat16 [1024, 1024], P('head'), may hold values from -0.75 to 0.75
Outputs:
- projected: bfloat16 [65536, 1024], P('seq', 'head')
The draws below stay inside these ranges and needn't reach their ends.
All inputs are finite; a program needn't handle non-finite values.
Results may differ from the reference program's by a relative error of at most 0.015.
Values may be sent and summed in bfloat16 or wider, within the bound.
No kernel may reach another device: no remote copies, remote signals or barrier semaphores. Data moves between devices by JAX's collectives and lax.ppermute only.
A program may use at most 64 MiB of HBM per device.

```python
import math
import jax
import jax.numpy as jnp
from jax import lax

D = 1024
HEADS = 16
HD = 64
BLOCK = 256
NB = 256
TOKENS = 65536


def draw_queries(key, part):
    field = jnp.clip(1.5 * jax.random.normal(jax.random.fold_in(key, 11), (TOKENS, D), jnp.float32), -6.0, 6.0)
    return field.astype(jnp.bfloat16)


def draw_keys(key, part):
    field = jnp.clip(1.5 * jax.random.normal(jax.random.fold_in(key, 13), (TOKENS, D), jnp.float32), -6.0, 6.0)
    return field.astype(jnp.bfloat16)


def touch_ends(array, stream_key, least, top_value):
    spot = [jax.random.randint(jax.random.fold_in(stream_key, axis), (), 0, length) for axis, length in enumerate(array.shape)]
    longest = array.shape.index(max(array.shape))
    next_to = spot[:longest] + [(spot[longest] + 1) % array.shape[longest]] + spot[longest + 1:]
    return array.at[tuple(spot)].set(least).at[tuple(next_to)].set(top_value)


def block_levels(own_key, shape, split, least, high):
    def one(axis_at, parts):
        heights = jax.random.uniform(jax.random.fold_in(jax.random.fold_in(own_key, 6), axis_at), (parts,), jnp.float32, least / len(split), high / len(split))
        return jnp.repeat(jnp.exp(heights), shape[axis_at] // parts).reshape((-1,) + (1,) * (len(shape) - axis_at - 1))

    gain = one(*split[0])
    for cut in split[1:]:
        gain = gain * one(*cut)
    return gain


def normal_values(key, shape, width, reach, pieces=(), held_as=jnp.bfloat16):
    gain = block_levels(key, shape, pieces, -0.22, 0.18) if pieces else 1.0
    values = jax.random.normal(key, shape, jnp.float32) * width * gain
    return jnp.minimum(jnp.maximum(values, -reach), reach).astype(held_as)


def setup_inputs(seed: int = 0) -> dict:
    key_list = jax.random.split(jax.random.key(seed), 6)
    queries = draw_queries(jax.random.fold_in(key_list[5], 71), 0)
    keys = draw_keys(jax.random.fold_in(key_list[5], 71), 0)
    values = normal_values(key_list[2], (TOKENS, D), 1.0, 6.0, ((0, 128), (1, 4)))
    block_keep = touch_ends((jax.random.randint(key_list[3], (NB,), 0, 4) < 3).astype(jnp.int32), jax.random.fold_in(key_list[3], 1), 0, 1)
    w_out = normal_values(key_list[4], (D, D), HD ** -0.5, 0.75, ((0, 4),))
    return dict(queries=queries, keys=keys, values=values, block_keep=block_keep, w_out=w_out)


def reference(queries, keys, values, block_keep, w_out):
    count = TOKENS // BLOCK
    levels = count.bit_length() - 1
    query_blocks = queries.reshape(count, BLOCK, HEADS, HD)
    key_blocks = keys.reshape(count, BLOCK, HEADS, HD)
    value_blocks = values.reshape(count, BLOCK, HEADS, HD)
    factor = 1.0 / math.sqrt(HD)

    def attend_block(index):
        listed = [index, index - 1, index + 1]
        for level in range(1, levels):
            listed.append(jnp.bitwise_xor(index, 1 << level))
        block_ids = jnp.stack(listed).astype(jnp.int32)
        inside = (block_ids >= 0) & (block_ids < count)
        safe_ids = jnp.clip(block_ids, 0, count - 1).astype(jnp.int32)
        allowed = inside & ((block_ids == index) | (block_keep[safe_ids] == 1))
        near_keys = key_blocks[safe_ids].astype(jnp.float32)
        near_values = value_blocks[safe_ids].astype(jnp.float32)
        query_now = lax.dynamic_index_in_dim(query_blocks, index, 0, keepdims=False).astype(jnp.float32)
        scores = jnp.einsum('qhd,skhd->hqsk', query_now, near_keys) * factor
        masked = jnp.where(allowed[None, None, :, None], scores, -jnp.inf)
        top = lax.optimization_barrier(jnp.max(masked, axis=(2, 3), keepdims=True))
        expo = jnp.exp(masked - top)
        total = lax.optimization_barrier(jnp.sum(expo, axis=(2, 3)))
        weights = expo.astype(jnp.bfloat16).astype(jnp.float32)
        mixed = jnp.einsum('hqsk,skhd->qhd', weights, near_values)
        mixed = mixed / jnp.transpose(total)[:, :, None]
        return mixed.reshape(BLOCK, HEADS * HD).astype(jnp.bfloat16)
    attended = lax.map(attend_block, jnp.arange(count, dtype=jnp.int32))
    attended = attended.reshape(TOKENS, HEADS * HD)
    return jnp.dot(attended, w_out, preferred_element_type=jnp.float32).astype(jnp.bfloat16)
```

```python
import math

import jax
import jax.numpy as jnp
from jax import lax
from jax.experimental import pallas as pl
from jax.experimental.pallas import tpu as pltpu
from jax.sharding import PartitionSpec as P

HD = 64
BLOCK = 256
MASKED = -1e30


def flat_exchange(value, axis, mask):
    pairs = [(source, source ^ mask) for source in range(lax.axis_size(axis))]
    return lax.ppermute(value, axis, pairs)


def halo_exchange(value, axis):
    count = lax.axis_size(axis)
    pairs = []
    for source in range(count):
        target = source + 1 if source % 2 else source - 1
        if 0 <= target < count:
            pairs.append((source, target))
    return lax.ppermute(value, axis, pairs)


def stacked_heads(q, heads):
    lane = lax.broadcasted_iota(jnp.int32, q.shape, 1)
    zero = jnp.zeros_like(q)
    return jnp.concatenate(
        [jnp.where((lane >= h * HD) & (lane < (h + 1) * HD), q, zero) for h in range(heads)], axis=0
    )


def fold(pieces, q, scores, scale, heads, m0, l0, acc0):
    qs = stacked_heads(q, heads)
    rows = qs.shape[0]
    half = rows // 2
    part = m0
    for at, (keys, _, bias) in enumerate(pieces):
        s = lax.dot_general(qs, keys(), (((1,), (1,)), ((), ())), preferred_element_type=jnp.float32)
        scores[at] = s
        top = jnp.maximum(s[:, :128], s[:, 128:]) + bias
        part = top if part is None else jnp.maximum(part, top)
    m = jnp.max(part, axis=1, keepdims=True)
    if l0 is None:
        total, acc_low, acc_high = None, None, None
    else:
        shrink = jnp.exp2((m0 - m) * scale)
        total = l0 * shrink
        acc_low = acc0[:half] * shrink[:half]
        acc_high = acc0[half:] * shrink[half:]
    for at, (_, values, bias) in enumerate(pieces):
        p = jnp.exp2((scores[at] - (m - bias)) * scale)
        add = p[:, :128] + p[:, 128:]
        total = add if total is None else total + add
        w = p.astype(jnp.bfloat16)
        v = values()
        low = jnp.dot(w[:half], v[:, :128], preferred_element_type=jnp.float32)
        high = jnp.dot(w[half:], v[:, 128:], preferred_element_type=jnp.float32)
        acc_low = low if acc_low is None else acc_low + low
        acc_high = high if acc_high is None else acc_high + high
    return m, total, jnp.concatenate([acc_low, acc_high], axis=0)


def bias_of(keep_ref, block, count):
    safe = jnp.clip(block, 0, count - 1)
    ok = (block >= 0) & (block < count) & (keep_ref[safe] == 1)
    return jnp.where(ok, 0.0, MASKED)


def early_kernel(scale, heads, bits, keep_ref, q_ref, own_ref, core_ref, halo_ref, *rest):
    far_refs = rest[: len(bits)]
    m_ref, l_ref, acc_ref, near, scores = rest[len(bits) :]
    count = keep_ref.shape[0]
    rank = lax.axis_index("seq")
    side = lax.rem(rank, 2)
    tokens = q_ref.shape[0]
    for local in range(2):
        other = 1 - local

        @pl.when(side == local)
        def _():
            near[local] = halo_ref[...]

        @pl.when(side != local)
        def _():
            near[local, :BLOCK] = core_ref[other * BLOCK : (other + 1) * BLOCK]
            near[local, BLOCK:] = core_ref[tokens + other * BLOCK : tokens + (other + 1) * BLOCK]

    def step(local, _):
        block = rank * 2 + local
        here = pl.multiple_of(local * BLOCK, BLOCK)
        there = pl.multiple_of((1 - local) * BLOCK, BLOCK)

        def of(ref, start):
            return (
                lambda: ref[pl.ds(start, BLOCK)],
                lambda: ref[pl.ds(pl.multiple_of(tokens + start, BLOCK), BLOCK)],
            )

        pieces = [
            (*of(own_ref, here), 0.0),
            (*of(own_ref, there), bias_of(keep_ref, block ^ 1, count)),
            (
                lambda: near[local, :BLOCK],
                lambda: near[local, BLOCK:],
                bias_of(keep_ref, block + 2 * local - 1, count),
            ),
            (*of(core_ref, here), bias_of(keep_ref, block ^ 2, count)),
        ]
        for ref, bit in zip(far_refs, bits, strict=True):
            pieces.append((*of(ref, here), bias_of(keep_ref, block ^ (1 << bit), count)))
        m, total, acc = fold(pieces, q_ref[pl.ds(here, BLOCK)], scores, scale, heads, None, None, None)
        m_ref[local] = jnp.broadcast_to(m, m_ref.shape[1:])
        l_ref[local] = total
        acc_ref[local] = acc
        return 0

    lax.fori_loop(0, 2, step, 0)


def late_kernel(scale, heads, bits, keep_ref, q_ref, m_ref, l_ref, acc_ref, *rest):
    far_refs = rest[: len(bits)]
    out_ref, scores = rest[len(bits) :]
    count = keep_ref.shape[0]
    rank = lax.axis_index("seq")
    tokens = q_ref.shape[0]

    def step(local, _):
        block = rank * 2 + local
        here = pl.multiple_of(local * BLOCK, BLOCK)
        pieces = []
        for ref, bit in zip(far_refs, bits, strict=True):
            pieces.append(
                (
                    lambda ref=ref: ref[pl.ds(here, BLOCK)],
                    lambda ref=ref: ref[pl.ds(pl.multiple_of(tokens + here, BLOCK), BLOCK)],
                    bias_of(keep_ref, block ^ (1 << bit), count),
                )
            )
        _, total, acc = fold(
            pieces, q_ref[pl.ds(here, BLOCK)], scores, scale, heads, m_ref[local], l_ref[local], acc_ref[local]
        )
        mixed = acc / jnp.sum(total, axis=1, keepdims=True)
        lane = lax.broadcasted_iota(jnp.int32, (BLOCK, 128), 1)
        for pair in range(2):
            first = mixed[2 * pair * BLOCK : (2 * pair + 1) * BLOCK]
            second = mixed[(2 * pair + 1) * BLOCK : (2 * pair + 2) * BLOCK]
            joined = jnp.where(lane < HD, first, second)
            out_ref[pl.ds(here, BLOCK), pair * 128 : (pair + 1) * 128] = joined.astype(out_ref.dtype)
        return 0

    lax.fori_loop(0, 2, step, 0)


def per_device(queries, keys, values, block_keep, w_out):
    rows, width = queries.shape
    heads = width // HD
    scale = 1.0 / math.sqrt(HD) * math.log2(math.e)
    packed = jnp.concatenate([keys, values], axis=0)
    far = {bit: flat_exchange(packed, "seq", 1 << (bit - 1)) for bit in (4, 3, 2, 6, 5, 7)}
    core = flat_exchange(packed, "seq", 1)
    side = lax.rem(lax.axis_index("seq"), 2)
    edge = packed.reshape(2, 2, BLOCK, width)
    edge = jnp.where(side == 1, edge[:, 1], edge[:, 0]).reshape(2 * BLOCK, width)
    halo = halo_exchange(edge, "seq")
    columns = lax.all_to_all(w_out, "head", 1, 0, tiled=True)

    vmem = pl.BlockSpec(memory_space=pltpu.VMEM)
    smem = pl.BlockSpec(memory_space=pltpu.SMEM)
    stacked = heads * BLOCK
    state = [jax.ShapeDtypeStruct((2, stacked, 128), jnp.float32)] * 3

    def cost(pieces):
        return pl.CostEstimate(
            flops=pieces * 4 * stacked * BLOCK * width,
            transcendentals=pieces * stacked * BLOCK,
            bytes_accessed=pieces * 2 * BLOCK * width * 2,
        )

    early_bits, late_bits = (5, 6, 7), (2, 3, 4)
    state = pl.pallas_call(
        lambda *refs: early_kernel(scale, heads, early_bits, *refs),
        out_shape=state,
        in_specs=[smem] + [vmem] * (4 + len(early_bits)),
        out_specs=[vmem] * 3,
        scratch_shapes=[
            pltpu.VMEM((2, 2 * BLOCK, width), jnp.bfloat16),
            pltpu.VMEM((4 + len(early_bits), stacked, BLOCK), jnp.float32),
        ],
        compiler_params=pltpu.CompilerParams(vmem_limit_bytes=32 << 20),
        cost_estimate=cost(2 * (4 + len(early_bits))),
        name="early",
    )(block_keep, queries, packed, core, halo, *[far[bit] for bit in early_bits])
    attended = pl.pallas_call(
        lambda *refs: late_kernel(scale, heads, late_bits, *refs),
        out_shape=jax.ShapeDtypeStruct((rows, width), jnp.bfloat16),
        in_specs=[smem] + [vmem] * (4 + len(late_bits)),
        out_specs=vmem,
        scratch_shapes=[pltpu.VMEM((len(late_bits), stacked, BLOCK), jnp.float32)],
        compiler_params=pltpu.CompilerParams(vmem_limit_bytes=32 << 20),
        cost_estimate=cost(2 * len(late_bits)),
        name="late",
    )(block_keep, queries, *state, *[far[bit] for bit in late_bits])
    gathered = lax.all_gather(attended, "head")
    weights = columns.reshape(-1, width, columns.shape[1])
    out = lax.dot_general(
        gathered, weights, (((0, 2), (0, 1)), ((), ())), preferred_element_type=jnp.float32
    )
    return out.astype(jnp.bfloat16)


def solution(mesh):
    placed = (P("seq", "head"), P("seq", "head"), P("seq", "head"), P(), P("head", None))
    return jax.shard_map(
        per_device, mesh=mesh, in_specs=placed, out_specs=P("seq", "head"), check_vma=False
    )
```

```python
import math

import jax
import jax.numpy as jnp
from jax import lax
from jax.experimental import pallas as pl
from jax.experimental.pallas import tpu as pltpu
from jax.sharding import PartitionSpec as P

HD = 64
BLOCK = 256
MASKED = -1e30


def flat_exchange(value, axis, mask):
    pairs = [(source, source ^ mask) for source in range(lax.axis_size(axis))]
    return lax.ppermute(value, axis, pairs)


def halo_exchange(value, axis):
    count = lax.axis_size(axis)
    pairs = []
    for source in range(count):
        target = source + 1 if source % 2 else source - 1
        if 0 <= target < count:
            pairs.append((source, target))
    return lax.ppermute(value, axis, pairs)


def after(value, *others):
    return lax.optimization_barrier((value, *others))[0]


def stacked_heads(q, heads):
    lane = lax.broadcasted_iota(jnp.int32, q.shape, 1)
    zero = jnp.zeros_like(q)
    return jnp.concatenate(
        [jnp.where((lane >= h * HD) & (lane < (h + 1) * HD), q, zero) for h in range(heads)], axis=0
    )


def fold(pieces, q, scores, scale, heads, m0, l0, acc0):
    qs = stacked_heads(q, heads)
    rows = qs.shape[0]
    half = rows // 2
    part = m0
    for at, (keys, _, bias) in enumerate(pieces):
        s = lax.dot_general(qs, keys(), (((1,), (1,)), ((), ())), preferred_element_type=jnp.float32)
        scores[at] = s
        top = jnp.maximum(s[:, :128], s[:, 128:]) + bias
        part = top if part is None else jnp.maximum(part, top)
    m = jnp.max(part, axis=1, keepdims=True)
    if l0 is None:
        total, acc_low, acc_high = None, None, None
    else:
        shrink = jnp.exp2((m0 - m) * scale)
        total = l0 * shrink
        acc_low = acc0[:half] * shrink[:half]
        acc_high = acc0[half:] * shrink[half:]
    for at, (_, values, bias) in enumerate(pieces):
        p = jnp.exp2((scores[at] - (m - bias)) * scale)
        add = p[:, :128] + p[:, 128:]
        total = add if total is None else total + add
        w = p.astype(jnp.bfloat16)
        v = values()
        low = jnp.dot(w[:half], v[:, :128], preferred_element_type=jnp.float32)
        high = jnp.dot(w[half:], v[:, 128:], preferred_element_type=jnp.float32)
        acc_low = low if acc_low is None else acc_low + low
        acc_high = high if acc_high is None else acc_high + high
    return m, total, jnp.concatenate([acc_low, acc_high], axis=0)


def bias_of(keep_ref, block, count):
    safe = jnp.clip(block, 0, count - 1)
    ok = (block >= 0) & (block < count) & (keep_ref[safe] == 1)
    return jnp.where(ok, 0.0, MASKED)


def part_of(ref, start):
    return (
        lambda: ref[pl.ds(start, BLOCK)],
        lambda: ref[pl.ds(pl.multiple_of(start + BLOCK, BLOCK), BLOCK)],
    )


def attend_kernel(scale, heads, local, plan, stateful, finish, keep_ref, q_ref, *refs):
    arrays = 1 + max(max(array) if isinstance(array, tuple) else array for _, array, _, _ in plan)
    sources, refs = refs[:arrays], refs[arrays:]
    m0, l0, acc0 = None, None, None
    if stateful:
        m0, l0, acc0 = (ref[...] for ref in refs[:3])
        refs = refs[3:]
    if finish:
        w_ref, out_ref, scores, near = refs
    else:
        m_ref, l_ref, acc_ref, scores, near = refs
    count = keep_ref.shape[0]
    rank = lax.axis_index("seq")
    block = rank * 2 + local
    pieces = []
    for what, array, start, number in plan:
        if what == "near":
            core_ref, halo_ref = sources[array[0]], sources[array[1]]
            mine = lax.rem(rank, 2) == local

            @pl.when(mine)
            def _():
                near[...] = halo_ref[...]

            @pl.when(jnp.logical_not(mine))
            def _():
                near[...] = core_ref[start : start + 2 * BLOCK]

            pieces.append((*part_of(near, 0), bias_of(keep_ref, block + number, count)))
        elif what == "self":
            pieces.append((*part_of(sources[array], start), 0.0))
        else:
            pieces.append((*part_of(sources[array], start), bias_of(keep_ref, block ^ number, count)))
    q = q_ref[local * BLOCK : (local + 1) * BLOCK]
    m, total, acc = fold(pieces, q, scores, scale, heads, m0, l0, acc0)
    if not finish:
        m_ref[...] = jnp.broadcast_to(m, m_ref.shape)
        l_ref[...] = total
        acc_ref[...] = acc
        return
    mixed = acc / jnp.sum(total, axis=1, keepdims=True)
    lane = lax.broadcasted_iota(jnp.int32, (BLOCK, 128), 1)
    joined = []
    for pair in range(2):
        first = mixed[2 * pair * BLOCK : (2 * pair + 1) * BLOCK]
        second = mixed[(2 * pair + 1) * BLOCK : (2 * pair + 2) * BLOCK]
        joined.append(jnp.where(lane < HD, first, second))
    attended = jnp.concatenate(joined, axis=1).astype(jnp.bfloat16)
    groups, _, columns = out_ref.shape
    for group in range(groups):
        w = w_ref[:, group * columns : (group + 1) * columns]
        out_ref[group] = jnp.dot(attended, w, preferred_element_type=jnp.float32).astype(out_ref.dtype)


def attend(name, block_keep, queries, local, sources, plan, state=None, w_out=None, groups=4):
    width = queries.shape[1]
    heads = width // HD
    stacked = heads * BLOCK
    scale = 1.0 / math.sqrt(HD) * math.log2(math.e)
    vmem = pl.BlockSpec(memory_space=pltpu.VMEM)
    smem = pl.BlockSpec(memory_space=pltpu.SMEM)
    finish = w_out is not None
    if finish:
        shape = jax.ShapeDtypeStruct((groups, BLOCK, w_out.shape[1] // groups), jnp.bfloat16)
        specs = vmem
    else:
        shape = [jax.ShapeDtypeStruct((stacked, 128), jnp.float32)] * 3
        specs = [vmem] * 3
    given = [block_keep, queries, *sources, *(state or ()), *((w_out,) if finish else ())]
    return pl.pallas_call(
        lambda *refs: attend_kernel(scale, heads, local, plan, state is not None, finish, *refs),
        out_shape=shape,
        in_specs=[smem] + [vmem] * (len(given) - 1),
        out_specs=specs,
        scratch_shapes=[
            pltpu.VMEM((len(plan), stacked, BLOCK), jnp.float32),
            pltpu.VMEM((2 * BLOCK, width), jnp.bfloat16),
        ],
        compiler_params=pltpu.CompilerParams(vmem_limit_bytes=18 << 20),
        cost_estimate=pl.CostEstimate(
            flops=len(plan) * 4 * stacked * BLOCK * width,
            transcendentals=len(plan) * stacked * BLOCK,
            bytes_accessed=len(plan) * 2 * BLOCK * width * 2,
        ),
        name=name,
    )(*given)


def per_device(queries, keys, values, block_keep, w_out):
    parts = [
        jnp.concatenate([keys[at : at + BLOCK], values[at : at + BLOCK]], axis=0) for at in (0, BLOCK)
    ]
    packed = jnp.concatenate(parts, axis=0)
    side = lax.rem(lax.axis_index("seq"), 2)
    edge = jnp.where(side == 1, parts[1], parts[0])
    y2 = [flat_exchange(part, "seq", 1 << 2) for part in parts]
    y1 = flat_exchange(packed, "seq", 1 << 1)
    x2 = flat_exchange(packed, "seq", 1 << 5)
    x1 = flat_exchange(packed, "seq", 1 << 4)
    y4 = [flat_exchange(part, "seq", (1 << 2) | (1 << 3)) for part in y2]
    core = flat_exchange(after(packed, x2), "seq", 1)
    z1 = flat_exchange(after(packed, x2), "seq", 1 << 6)
    halo = halo_exchange(after(edge, x1), "seq")

    full = [packed, core, halo, y1, x1, x2, z1]

    def common(local):
        here, there = 2 * BLOCK * local, 2 * BLOCK * (1 - local)
        return [
            ("self", 0, here, 0),
            ("xor", 0, there, 1),
            ("near", (1, 2), there, 2 * local - 1),
            ("xor", 1, here, 2),
            ("xor", 3, here, 4),
            ("xor", 4, here, 32),
            ("xor", 5, here, 64),
            ("xor", 6, here, 128),
        ]

    first = attend(
        "first",
        block_keep,
        after(queries, y2[1]),
        0,
        full + [y2[0], y4[0]],
        common(0) + [("xor", 7, 0, 8), ("xor", 8, 0, 16)],
        w_out=w_out,
    )
    out0 = lax.psum_scatter(first, "head", scatter_dimension=0, tiled=False)
    state = attend(
        "second", block_keep, after(queries, first), 1, full + [y2[1]], common(1) + [("xor", 7, 0, 8)]
    )
    last = attend(
        "last", block_keep, queries, 1, [y4[1]], [("xor", 0, 0, 16)], state=state, w_out=w_out
    )
    spread = lax.all_to_all(last, "head", 0, 0, tiled=False)
    out1 = jnp.sum(spread.astype(jnp.float32), axis=0).astype(jnp.bfloat16)
    return jnp.concatenate([out0, out1], axis=0)


def solution(mesh):
    placed = (P("seq", "head"), P("seq", "head"), P("seq", "head"), P(), P("head", None))
    return jax.shard_map(
        per_device, mesh=mesh, in_specs=placed, out_specs=P("seq", "head"), check_vma=False
    )
```

```python
import math

import jax
import jax.numpy as jnp
from jax import lax
from jax.experimental import pallas as pl
from jax.experimental.pallas import tpu as pltpu
from jax.sharding import PartitionSpec as P

HD = 64
BLOCK = 256
MASKED = -1e30


def flat_exchange(value, axis, mask):
    pairs = [(source, source ^ mask) for source in range(lax.axis_size(axis))]
    return lax.ppermute(value, axis, pairs)


def halo_exchange(value, axis):
    count = lax.axis_size(axis)
    pairs = []
    for source in range(count):
        target = source + 1 if source % 2 else source - 1
        if 0 <= target < count:
            pairs.append((source, target))
    return lax.ppermute(value, axis, pairs)


def after(value, *others):
    return lax.optimization_barrier((value, *others))[0]


def stacked_heads(q, heads):
    lane = lax.broadcasted_iota(jnp.int32, q.shape, 1)
    zero = jnp.zeros_like(q)
    return jnp.concatenate(
        [jnp.where((lane >= h * HD) & (lane < (h + 1) * HD), q, zero) for h in range(heads)], axis=0
    )


def fold(pieces, q, scores, scale, heads, m0, l0, acc0):
    qs = stacked_heads(q, heads)
    rows = qs.shape[0]
    half = rows // 2
    part = m0
    for at, (keys, _, bias) in enumerate(pieces):
        s = lax.dot_general(qs, keys(), (((1,), (1,)), ((), ())), preferred_element_type=jnp.float32)
        scores[at] = s
        top = jnp.maximum(s[:, :128], s[:, 128:]) + bias
        part = top if part is None else jnp.maximum(part, top)
    m = jnp.max(part, axis=1, keepdims=True)
    if l0 is None:
        total, acc_low, acc_high = None, None, None
    else:
        shrink = jnp.exp2((m0 - m) * scale)
        total = l0 * shrink
        acc_low = acc0[:half] * shrink[:half]
        acc_high = acc0[half:] * shrink[half:]
    for at, (_, values, bias) in enumerate(pieces):
        p = jnp.exp2((scores[at] - (m - bias)) * scale)
        add = p[:, :128] + p[:, 128:]
        total = add if total is None else total + add
        w = p.astype(jnp.bfloat16)
        v = values()
        low = jnp.dot(w[:half], v[:, :128], preferred_element_type=jnp.float32)
        high = jnp.dot(w[half:], v[:, 128:], preferred_element_type=jnp.float32)
        acc_low = low if acc_low is None else acc_low + low
        acc_high = high if acc_high is None else acc_high + high
    return m, total, jnp.concatenate([acc_low, acc_high], axis=0)


def bias_of(keep_ref, block, count):
    safe = jnp.clip(block, 0, count - 1)
    ok = (block >= 0) & (block < count) & (keep_ref[safe] == 1)
    return jnp.where(ok, 0.0, MASKED)


def part_of(ref, start):
    return (
        lambda: ref[pl.ds(start, BLOCK)],
        lambda: ref[pl.ds(pl.multiple_of(start + BLOCK, BLOCK), BLOCK)],
    )


def attend_kernel(scale, heads, local, plan, stateful, finish, rotated, keep_ref, q_ref, *refs):
    arrays = 1 + max(max(array) if isinstance(array, tuple) else array for _, array, _, _ in plan)
    sources, refs = refs[:arrays], refs[arrays:]
    m0, l0, acc0 = None, None, None
    if stateful:
        m0, l0, acc0 = (ref[...] for ref in refs[:3])
        refs = refs[3:]
    if finish:
        w_ref, *outs, scores, near = refs
        out_refs = outs if rotated else [outs[0].at[at] for at in range(outs[0].shape[0])]
    else:
        m_ref, l_ref, acc_ref, scores, near = refs
    count = keep_ref.shape[0]
    rank = lax.axis_index("seq")
    block = rank * 2 + local
    pieces = []
    for what, array, start, number in plan:
        if what == "near":
            core_ref, halo_ref = sources[array[0]], sources[array[1]]
            mine = lax.rem(rank, 2) == local

            @pl.when(mine)
            def _():
                near[...] = halo_ref[...]

            @pl.when(jnp.logical_not(mine))
            def _():
                near[...] = core_ref[start : start + 2 * BLOCK]

            pieces.append((*part_of(near, 0), bias_of(keep_ref, block + number, count)))
        elif what == "self":
            pieces.append((*part_of(sources[array], start), 0.0))
        else:
            pieces.append((*part_of(sources[array], start), bias_of(keep_ref, block ^ number, count)))
    q = q_ref[local * BLOCK : (local + 1) * BLOCK]
    m, total, acc = fold(pieces, q, scores, scale, heads, m0, l0, acc0)
    if not finish:
        m_ref[...] = jnp.broadcast_to(m, m_ref.shape)
        l_ref[...] = total
        acc_ref[...] = acc
        return
    mixed = acc / jnp.sum(total, axis=1, keepdims=True)
    lane = lax.broadcasted_iota(jnp.int32, (BLOCK, 128), 1)
    joined = []
    for pair in range(2):
        first = mixed[2 * pair * BLOCK : (2 * pair + 1) * BLOCK]
        second = mixed[(2 * pair + 1) * BLOCK : (2 * pair + 2) * BLOCK]
        joined.append(jnp.where(lane < HD, first, second))
    attended = jnp.concatenate(joined, axis=1).astype(jnp.bfloat16)
    groups = len(out_refs)
    columns = out_refs[0].shape[1]
    for group, out_ref in enumerate(out_refs):
        start = group * columns
        if rotated:
            start = pl.multiple_of(lax.rem(lax.axis_index("head") + group, groups) * columns, columns)
        w = w_ref[:, pl.ds(start, columns)]
        out_ref[...] = jnp.dot(attended, w, preferred_element_type=jnp.float32).astype(out_ref.dtype)


def attend(name, block_keep, queries, local, sources, plan, state=None, w_out=None, rotated=False):
    width = queries.shape[1]
    heads = width // HD
    stacked = heads * BLOCK
    scale = 1.0 / math.sqrt(HD) * math.log2(math.e)
    vmem = pl.BlockSpec(memory_space=pltpu.VMEM)
    smem = pl.BlockSpec(memory_space=pltpu.SMEM)
    finish = w_out is not None
    if finish:
        groups = lax.axis_size("head")
        columns = w_out.shape[1] // groups
        if rotated:
            shape = [jax.ShapeDtypeStruct((BLOCK, columns), jnp.bfloat16)] * groups
            specs = [vmem] * groups
        else:
            shape = jax.ShapeDtypeStruct((groups, BLOCK, columns), jnp.bfloat16)
            specs = vmem
    else:
        shape = [jax.ShapeDtypeStruct((stacked, 128), jnp.float32)] * 3
        specs = [vmem] * 3
    given = [block_keep, queries, *sources, *(state or ()), *((w_out,) if finish else ())]
    return pl.pallas_call(
        lambda *refs: attend_kernel(scale, heads, local, plan, state is not None, finish, rotated, *refs),
        out_shape=shape,
        in_specs=[smem] + [vmem] * (len(given) - 1),
        out_specs=specs,
        scratch_shapes=[
            pltpu.VMEM((len(plan), stacked, BLOCK), jnp.float32),
            pltpu.VMEM((2 * BLOCK, width), jnp.bfloat16),
        ],
        compiler_params=pltpu.CompilerParams(vmem_limit_bytes=(len(plan) + 7) << 20),
        cost_estimate=pl.CostEstimate(flops=1 << 20, transcendentals=0, bytes_accessed=1 << 14),
        name=name,
    )(*given)


def per_device(queries, keys, values, block_keep, w_out):
    parts = [
        jnp.concatenate([keys[at : at + BLOCK], values[at : at + BLOCK]], axis=0) for at in (0, BLOCK)
    ]
    packed = jnp.concatenate(parts, axis=0)
    side = lax.rem(lax.axis_index("seq"), 2)
    edge = jnp.where(side == 1, parts[1], parts[0])
    y2 = flat_exchange(packed, "seq", 1 << 2)
    y4a = flat_exchange(parts[0], "seq", 1 << 3)
    y1 = flat_exchange(packed, "seq", 1 << 1)
    core = flat_exchange(packed, "seq", 1)
    x2 = flat_exchange(packed, "seq", 1 << 5)
    x1 = flat_exchange(after(packed, core), "seq", 1 << 4)
    z1 = flat_exchange(after(packed, x2), "seq", 1 << 6)
    halo = halo_exchange(after(edge, core), "seq")
    y4b = flat_exchange(after(parts[1], y1), "seq", 1 << 3)

    def early(local, queries):
        here, there = 2 * BLOCK * local, 2 * BLOCK * (1 - local)
        plan = [
            ("self", 0, here, 0),
            ("xor", 0, there, 1),
            ("xor", 1, here, 2),
            ("xor", 2, here, 4),
            ("xor", 3, here, 8),
            ("xor", 4, here, 32),
            ("xor", 5, here, 64),
        ]
        sources = [packed, core, y1, y2, x1, x2]
        return attend(f"early{local}", block_keep, queries, local, sources, plan)

    def late(local, y4, state, queries, rotated):
        here, there = 2 * BLOCK * local, 2 * BLOCK * (1 - local)
        plan = [("near", (0, 1), there, 2 * local - 1), ("xor", 2, here, 128), ("xor", 3, 0, 16)]
        sources = [core, halo, z1, y4]
        return attend(
            f"late{local}",
            block_keep,
            queries,
            local,
            sources,
            plan,
            state=state,
            w_out=w_out,
            rotated=rotated,
        )

    state0 = early(0, queries)
    state1 = early(1, queries)
    mine, *pieces = late(0, y4a, state0, after(queries, state1[0]), True)
    groups = 1 + len(pieces)
    moved = [
        lax.ppermute(piece, "head", [(h, (h + hop + 1) % groups) for h in range(groups)])
        for hop, piece in enumerate(pieces)
    ]
    shares = late(1, y4b, state1, after(queries, mine), False)
    spread = lax.all_to_all(after(shares, *moved), "head", 0, 0, tiled=False)
    total = mine.astype(jnp.float32)
    for piece in moved:
        total = total + piece.astype(jnp.float32)
    outs = [total, jnp.sum(spread.astype(jnp.float32), axis=0)]
    return jnp.concatenate([out.astype(jnp.bfloat16) for out in outs], axis=0)


def solution(mesh):
    placed = (P("seq", "head"), P("seq", "head"), P("seq", "head"), P(), P("head", None))
    return jax.shard_map(
        per_device, mesh=mesh, in_specs=placed, out_specs=P("seq", "head"), check_vma=False
    )
```

```python
import math

import jax
import jax.numpy as jnp
from jax import lax
from jax.experimental import pallas as pl
from jax.experimental.pallas import tpu as pltpu
from jax.sharding import PartitionSpec as P

HD = 64
BLOCK = 256
PAIR = 2 * BLOCK
MASKED = -1e30
COST = 4


def flat_exchange(value, axis, mask):
    pairs = [(source, source ^ mask) for source in range(lax.axis_size(axis))]
    return lax.ppermute(value, axis, pairs)


def halo_exchange(value, axis):
    count = lax.axis_size(axis)
    pairs = []
    for source in range(count):
        target = source + 1 if source % 2 else source - 1
        if 0 <= target < count:
            pairs.append((source, target))
    return lax.ppermute(value, axis, pairs)


def crosswise(value, axis, bits):
    mask = sum(1 << bit for bit in bits)
    groups = []
    for base in range(lax.axis_size(axis)):
        if base & mask == 0:
            groups.append([base | (i << bits[0]) for i in range(1 << len(bits))])
    return lax.all_gather(value, axis, axis_index_groups=groups)


def after(value, *others):
    return lax.optimization_barrier((value, *others))[0]


def stacked_heads(q, heads):
    lane = lax.broadcasted_iota(jnp.int32, q.shape, 1)
    zero = jnp.zeros_like(q)
    return jnp.concatenate(
        [jnp.where((lane >= h * HD) & (lane < (h + 1) * HD), q, zero) for h in range(heads)], axis=0
    )


def fold(pieces, q, scores, scale, heads, before):
    qs = stacked_heads(q, heads)
    half = qs.shape[0] // 2
    part = None
    for at, (keys, _, bias) in enumerate(pieces):
        s = lax.dot_general(qs, keys(), (((1,), (1,)), ((), ())), preferred_element_type=jnp.float32)
        scores[at] = s
        top = jnp.maximum(s[:, :128], s[:, 128:]) + bias
        part = top if part is None else jnp.maximum(part, top)
    total, acc_low, acc_high = None, None, None
    if before is None:
        m = jnp.max(part, axis=1, keepdims=True)
    else:
        m0, l0, acc0 = before()
        m = jnp.max(jnp.maximum(part, m0), axis=1, keepdims=True)
        shrink = jnp.exp2((m0 - m) * scale)
        total = l0 * shrink
        acc_low = acc0[:half] * shrink[:half]
        acc_high = acc0[half:] * shrink[half:]
    for at, (_, values, bias) in enumerate(pieces):
        p = jnp.exp2((scores[at] - (m - bias)) * scale)
        add = p[:, :128] + p[:, 128:]
        total = add if total is None else total + add
        w = p.astype(jnp.bfloat16)
        v = values()
        low = jnp.dot(w[:half], v[:, :128], preferred_element_type=jnp.float32)
        high = jnp.dot(w[half:], v[:, 128:], preferred_element_type=jnp.float32)
        acc_low = low if acc_low is None else acc_low + low
        acc_high = high if acc_high is None else acc_high + high
    return m, total, jnp.concatenate([acc_low, acc_high], axis=0)


def bias_of(keep_ref, block, count):
    safe = jnp.clip(block, 0, count - 1)
    ok = (block >= 0) & (block < count) & (keep_ref[safe] == 1)
    return jnp.where(ok, 0.0, MASKED)


def attend_kernel(scale, heads, local, plan, arrays, stateful, finish, keep_ref, q_ref, *refs):
    sources, refs = refs[:arrays], refs[arrays:]
    state, w_hbm = None, None
    if stateful:
        state, refs = refs[0], refs[1:]
    if finish:
        w_hbm, out_ref, *refs = refs
    else:
        state_out, *refs = refs
    scores, held, q_held, extra, sems = refs
    count = keep_ref.shape[0]
    rank = lax.axis_index("seq")
    block = rank * 2 + local
    q_copy = pltpu.make_async_copy(q_ref.at[pl.ds(local * BLOCK, BLOCK)], q_held, sems.at[len(plan)])
    q_copy.start()
    copies, biases = [], []
    for at, (what, array, start, number) in enumerate(plan):
        rows = pl.ds(start, PAIR)
        bias = 0.0
        if what == "near":
            mine = lax.rem(rank, 2) == local
            kept = pltpu.make_async_copy(sources[array[1]], held.at[at], sems.at[at])
            shared = pltpu.make_async_copy(sources[array[0]].at[rows], held.at[at], sems.at[at])
            pl.when(mine)(kept.start)
            pl.when(jnp.logical_not(mine))(shared.start)
            copies.append(kept)
            bias = bias_of(keep_ref, block + number, count)
        else:
            source = sources[array]
            if what == "across":
                crossed, level = number
                place = lax.rem(rank >> level, source.shape[0]) ^ crossed
                source = source.at[place]
                number = crossed << (level + 1)
            copies.append(pltpu.make_async_copy(source.at[rows], held.at[at], sems.at[at]))
            copies[-1].start()
            if what != "self":
                bias = bias_of(keep_ref, block ^ number, count)
        biases.append(bias)
    if stateful:
        state_copy = pltpu.make_async_copy(state, extra, sems.at[len(plan) + 1])
        state_copy.start()

    def keys_of(at):
        copies[at].wait()
        return held[at, :BLOCK]

    def before():
        state_copy.wait()
        return extra[0], extra[1], extra[2]

    pieces = [
        (lambda at=at: keys_of(at), lambda at=at: held[at, BLOCK:], biases[at]) for at in range(len(plan))
    ]
    q_copy.wait()
    m, total, acc = fold(pieces, q_held[...], scores, scale, heads, before if stateful else None)
    if not finish:
        extra[0] = jnp.broadcast_to(m, extra.shape[1:])
        extra[1] = total
        extra[2] = acc
        out_copy = pltpu.make_async_copy(extra, state_out, sems.at[len(plan) + 1])
        out_copy.start()
        out_copy.wait()
        return
    mixed = acc / jnp.sum(total, axis=1, keepdims=True)
    lane = lax.broadcasted_iota(jnp.int32, (BLOCK, 128), 1)
    joined = []
    for pair in range(2):
        first = mixed[2 * pair * BLOCK : (2 * pair + 1) * BLOCK]
        second = mixed[(2 * pair + 1) * BLOCK : (2 * pair + 2) * BLOCK]
        joined.append(jnp.where(lane < HD, first, second))
    attended = jnp.concatenate(joined, axis=1).astype(jnp.bfloat16)
    columns = out_ref.shape[2]
    for group in range(out_ref.shape[0]):
        w = w_hbm[:, group * columns : (group + 1) * columns]
        out_ref[group] = jnp.dot(attended, w, preferred_element_type=jnp.float32).astype(out_ref.dtype)


def attend(name, block_keep, queries, local, sources, plan, state=None, w_out=None):
    width = queries.shape[1]
    heads = width // HD
    stacked = heads * BLOCK
    scale = 1.0 / math.sqrt(HD) * math.log2(math.e)
    vmem = pl.BlockSpec(memory_space=pltpu.VMEM)
    smem = pl.BlockSpec(memory_space=pltpu.SMEM)
    hbm = pl.BlockSpec(memory_space=pltpu.HBM)
    finish = w_out is not None
    if finish:
        groups = lax.axis_size("head")
        shape = jax.ShapeDtypeStruct((groups, BLOCK, w_out.shape[1] // groups), jnp.bfloat16)
    else:
        shape = pltpu.HBM((3, stacked, 128), jnp.float32)
    far = [queries, *sources] if state is None else [queries, *sources, state]
    given = [block_keep, *(pltpu.with_memory_space_constraint(x, pltpu.HBM) for x in far)]
    specs = [smem] + [hbm] * len(far)
    if finish:
        given, specs = given + [w_out], specs + [vmem]
    return pl.pallas_call(
        lambda *refs: attend_kernel(
            scale, heads, local, plan, len(sources), state is not None, finish, *refs
        ),
        out_shape=shape,
        in_specs=specs,
        out_specs=vmem if finish else hbm,
        scratch_shapes=[
            pltpu.VMEM((len(plan), stacked, BLOCK), jnp.float32),
            pltpu.VMEM((len(plan), PAIR, width), jnp.bfloat16),
            pltpu.VMEM((BLOCK, width), jnp.bfloat16),
            pltpu.VMEM((3, stacked, 128), jnp.float32),
            pltpu.SemaphoreType.DMA((len(plan) + 2,)),
        ],
        compiler_params=pltpu.CompilerParams(vmem_limit_bytes=(2 * len(plan) + 12) << 20),
        cost_estimate=pl.CostEstimate(
            flops=len(plan) * 4 * stacked * BLOCK * width * COST,
            transcendentals=len(plan) * stacked * BLOCK,
            bytes_accessed=len(plan) * 2 * BLOCK * width * 2,
        ),
        name=name,
    )(*given)


def per_device(queries, keys, values, block_keep, w_out):
    parts = [
        jnp.concatenate([keys[at : at + BLOCK], values[at : at + BLOCK]], axis=0) for at in (0, BLOCK)
    ]
    packed = jnp.concatenate(parts, axis=0)
    side = lax.rem(lax.axis_index("seq"), 2)
    edge = jnp.where(side == 1, parts[1], parts[0])
    xs = crosswise(packed, "seq", (4, 5))
    y2a = flat_exchange(parts[0], "seq", 1 << 2)
    y2b = flat_exchange(after(parts[1], y2a), "seq", 1 << 2)
    y4a = flat_exchange(y2a, "seq", (1 << 2) | (1 << 3))
    y4b = flat_exchange(y2b, "seq", (1 << 2) | (1 << 3))
    core = flat_exchange(packed, "seq", 1)
    y1 = flat_exchange(packed, "seq", 1 << 1)
    z1 = flat_exchange(after(packed, core), "seq", 1 << 6)
    halo = halo_exchange(after(edge, y2a), "seq")
    y2, y4 = [y2a, y2b], [y4a, y4b]

    def early(local, queries):
        here, there = PAIR * local, PAIR * (1 - local)
        plan = [
            ("self", 0, here, 0),
            ("xor", 0, there, 1),
            ("xor", 1, here, 2),
            ("xor", 2, here, 4),
        ]
        return attend(f"early{local}", block_keep, queries, local, [packed, core, y1], plan)

    def late(local, state, queries):
        here, there = PAIR * local, PAIR * (1 - local)
        plan = [
            ("near", (0, 1), there, 2 * local - 1),
            ("xor", 2, here, 128),
            ("across", 3, here, (1, 4)),
            ("across", 3, here, (2, 4)),
            ("xor", 4, 0, 8),
            ("xor", 5, 0, 16),
        ]
        sources = [core, halo, z1, xs, y2[local], y4[local]]
        return attend(
            f"late{local}", block_keep, queries, local, sources, plan, state=state, w_out=w_out
        )

    state0 = early(0, queries)
    state1 = early(1, queries)
    shares0 = late(0, state0, after(queries, state1))
    out0 = lax.psum_scatter(shares0, "head", scatter_dimension=0, tiled=False)
    shares1 = late(1, state1, after(queries, shares0))
    spread = lax.all_to_all(shares1, "head", 0, 0, tiled=False)
    out1 = jnp.sum(spread.astype(jnp.float32), axis=0).astype(jnp.bfloat16)
    return jnp.concatenate([out0, out1], axis=0)


def solution(mesh):
    placed = (P("seq", "head"), P("seq", "head"), P("seq", "head"), P(), P("head", None))
    return jax.shard_map(
        per_device, mesh=mesh, in_specs=placed, out_specs=P("seq", "head"), check_vma=False
    )
```

```python
import math

import jax
import jax.numpy as jnp
from jax import lax
from jax.experimental import pallas as pl
from jax.experimental.pallas import tpu as pltpu
from jax.sharding import PartitionSpec as P

HD = 64
BLOCK = 256
MASKED = -1e30
COST = 4


def flat_exchange(value, axis, mask):
    pairs = [(source, source ^ mask) for source in range(lax.axis_size(axis))]
    return lax.ppermute(value, axis, pairs)


def halo_exchange(value, axis):
    count = lax.axis_size(axis)
    pairs = []
    for source in range(count):
        target = source + 1 if source % 2 else source - 1
        if 0 <= target < count:
            pairs.append((source, target))
    return lax.ppermute(value, axis, pairs)


def after(value, *others):
    return lax.optimization_barrier((value, *others))[0]


def stacked_heads(q, heads):
    lane = lax.broadcasted_iota(jnp.int32, q.shape, 1)
    zero = jnp.zeros_like(q)
    return jnp.concatenate(
        [jnp.where((lane >= h * HD) & (lane < (h + 1) * HD), q, zero) for h in range(heads)], axis=0
    )


def fold(pieces, q, scores, scale, heads, m0, l0, acc0):
    qs = stacked_heads(q, heads)
    rows = qs.shape[0]
    half = rows // 2
    part = m0
    for at, (keys, _, bias) in enumerate(pieces):
        s = lax.dot_general(qs, keys(), (((1,), (1,)), ((), ())), preferred_element_type=jnp.float32)
        scores[at] = s
        top = jnp.maximum(s[:, :128], s[:, 128:]) + bias
        part = top if part is None else jnp.maximum(part, top)
    m = jnp.max(part, axis=1, keepdims=True)
    if l0 is None:
        total, acc_low, acc_high = None, None, None
    else:
        shrink = jnp.exp2((m0 - m) * scale)
        total = l0 * shrink
        acc_low = acc0[:half] * shrink[:half]
        acc_high = acc0[half:] * shrink[half:]
    for at, (_, values, bias) in enumerate(pieces):
        p = jnp.exp2((scores[at] - (m - bias)) * scale)
        add = p[:, :128] + p[:, 128:]
        total = add if total is None else total + add
        w = p.astype(jnp.bfloat16)
        v = values()
        low = jnp.dot(w[:half], v[:, :128], preferred_element_type=jnp.float32)
        high = jnp.dot(w[half:], v[:, 128:], preferred_element_type=jnp.float32)
        acc_low = low if acc_low is None else acc_low + low
        acc_high = high if acc_high is None else acc_high + high
    return m, total, jnp.concatenate([acc_low, acc_high], axis=0)


def bias_of(keep_ref, block, count):
    safe = jnp.clip(block, 0, count - 1)
    ok = (block >= 0) & (block < count) & (keep_ref[safe] == 1)
    return jnp.where(ok, 0.0, MASKED)


def part_of(ref, start):
    return (
        lambda: ref[pl.ds(start, BLOCK)],
        lambda: ref[pl.ds(pl.multiple_of(start + BLOCK, BLOCK), BLOCK)],
    )


def attend_kernel(scale, heads, local, plan, stateful, finish, rotated, keep_ref, q_ref, *refs):
    arrays = 1 + max(max(array) if isinstance(array, tuple) else array for _, array, _, _ in plan)
    sources, refs = refs[:arrays], refs[arrays:]
    m0, l0, acc0 = None, None, None
    if stateful:
        m0, l0, acc0 = (ref[...] for ref in refs[:3])
        refs = refs[3:]
    if finish:
        w_ref, *outs, scores, near = refs
        out_refs = outs if rotated else [outs[0].at[at] for at in range(outs[0].shape[0])]
    else:
        m_ref, l_ref, acc_ref, scores, near = refs
    count = keep_ref.shape[0]
    rank = lax.axis_index("seq")
    block = rank * 2 + local
    pieces = []
    for what, array, start, number in plan:
        if what == "near":
            core_ref, halo_ref = sources[array[0]], sources[array[1]]
            mine = lax.rem(rank, 2) == local

            @pl.when(mine)
            def _():
                near[...] = halo_ref[...]

            @pl.when(jnp.logical_not(mine))
            def _():
                near[...] = core_ref[start : start + 2 * BLOCK]

            pieces.append((*part_of(near, 0), bias_of(keep_ref, block + number, count)))
        elif what == "self":
            pieces.append((*part_of(sources[array], start), 0.0))
        else:
            pieces.append((*part_of(sources[array], start), bias_of(keep_ref, block ^ number, count)))
    q = q_ref[local * BLOCK : (local + 1) * BLOCK]
    m, total, acc = fold(pieces, q, scores, scale, heads, m0, l0, acc0)
    if not finish:
        m_ref[...] = jnp.broadcast_to(m, m_ref.shape)
        l_ref[...] = total
        acc_ref[...] = acc
        return
    mixed = acc / jnp.sum(total, axis=1, keepdims=True)
    lane = lax.broadcasted_iota(jnp.int32, (BLOCK, 128), 1)
    joined = []
    for pair in range(2):
        first = mixed[2 * pair * BLOCK : (2 * pair + 1) * BLOCK]
        second = mixed[(2 * pair + 1) * BLOCK : (2 * pair + 2) * BLOCK]
        joined.append(jnp.where(lane < HD, first, second))
    attended = jnp.concatenate(joined, axis=1).astype(jnp.bfloat16)
    groups = len(out_refs)
    columns = out_refs[0].shape[1]
    for group, out_ref in enumerate(out_refs):
        start = group * columns
        if rotated:
            start = pl.multiple_of(lax.rem(lax.axis_index("head") + group, groups) * columns, columns)
        w = w_ref[:, pl.ds(start, columns)]
        out_ref[...] = jnp.dot(attended, w, preferred_element_type=jnp.float32).astype(out_ref.dtype)


def attend(name, block_keep, queries, local, sources, plan, state=None, w_out=None, rotated=False):
    width = queries.shape[1]
    heads = width // HD
    stacked = heads * BLOCK
    scale = 1.0 / math.sqrt(HD) * math.log2(math.e)
    vmem = pl.BlockSpec(memory_space=pltpu.VMEM)
    smem = pl.BlockSpec(memory_space=pltpu.SMEM)
    finish = w_out is not None
    if finish:
        groups = lax.axis_size("head")
        columns = w_out.shape[1] // groups
        if rotated:
            shape = [jax.ShapeDtypeStruct((BLOCK, columns), jnp.bfloat16)] * groups
            specs = [vmem] * groups
        else:
            shape = jax.ShapeDtypeStruct((groups, BLOCK, columns), jnp.bfloat16)
            specs = vmem
    else:
        shape = [jax.ShapeDtypeStruct((stacked, 128), jnp.float32)] * 3
        specs = [vmem] * 3
    given = [block_keep, queries, *sources, *(state or ()), *((w_out,) if finish else ())]
    return pl.pallas_call(
        lambda *refs: attend_kernel(scale, heads, local, plan, state is not None, finish, rotated, *refs),
        out_shape=shape,
        in_specs=[smem] + [vmem] * (len(given) - 1),
        out_specs=specs,
        scratch_shapes=[
            pltpu.VMEM((len(plan), stacked, BLOCK), jnp.float32),
            pltpu.VMEM((2 * BLOCK, width), jnp.bfloat16),
        ],
        compiler_params=pltpu.CompilerParams(vmem_limit_bytes=(len(plan) + 7) << 20),
        cost_estimate=pl.CostEstimate(
            flops=len(plan) * 4 * stacked * BLOCK * width * COST,
            transcendentals=len(plan) * stacked * BLOCK,
            bytes_accessed=len(plan) * 2 * BLOCK * width * 2,
        ),
        name=name,
    )(*given)


def per_device(queries, keys, values, block_keep, w_out):
    parts = [
        jnp.concatenate([keys[at : at + BLOCK], values[at : at + BLOCK]], axis=0) for at in (0, BLOCK)
    ]
    packed = jnp.concatenate(parts, axis=0)
    side = lax.rem(lax.axis_index("seq"), 2)
    edge = jnp.where(side == 1, parts[1], parts[0])
    y2 = flat_exchange(packed, "seq", 1 << 2)
    y4a = flat_exchange(parts[0], "seq", 1 << 3)
    y1 = flat_exchange(packed, "seq", 1 << 1)
    core = flat_exchange(packed, "seq", 1)
    x2 = flat_exchange(packed, "seq", 1 << 5)
    x1 = flat_exchange(after(packed, core), "seq", 1 << 4)
    z1 = flat_exchange(after(packed, x2), "seq", 1 << 6)
    halo = halo_exchange(after(edge, core), "seq")
    y4b = flat_exchange(after(parts[1], y1), "seq", 1 << 3)

    def early(local, queries):
        here, there = 2 * BLOCK * local, 2 * BLOCK * (1 - local)
        plan = [
            ("self", 0, here, 0),
            ("xor", 0, there, 1),
            ("xor", 1, here, 2),
            ("xor", 2, here, 4),
            ("xor", 3, here, 32),
            ("xor", 4, here, 64),
        ]
        sources = [packed, core, y1, x1, x2]
        return attend(f"early{local}", block_keep, queries, local, sources, plan)

    def late(local, y4, state, queries, rotated):
        here, there = 2 * BLOCK * local, 2 * BLOCK * (1 - local)
        plan = [
            ("near", (0, 1), there, 2 * local - 1),
            ("xor", 2, here, 128),
            ("xor", 3, here, 8),
            ("xor", 4, 0, 16),
        ]
        sources = [core, halo, z1, y2, y4]
        return attend(
            f"late{local}",
            block_keep,
            queries,
            local,
            sources,
            plan,
            state=state,
            w_out=w_out,
            rotated=rotated,
        )

    state0 = early(0, queries)
    state1 = early(1, queries)
    mine, *pieces = late(0, y4a, state0, after(queries, state1[0]), True)
    groups = 1 + len(pieces)
    moved = [
        lax.ppermute(piece, "head", [(h, (h + hop + 1) % groups) for h in range(groups)])
        for hop, piece in enumerate(pieces)
    ]
    shares = late(1, y4b, state1, after(queries, mine), False)
    spread = lax.all_to_all(after(shares, *moved), "head", 0, 0, tiled=False)
    total = mine.astype(jnp.float32)
    for piece in moved:
        total = total + piece.astype(jnp.float32)
    outs = [total, jnp.sum(spread.astype(jnp.float32), axis=0)]
    return jnp.concatenate([out.astype(jnp.bfloat16) for out in outs], axis=0)


def solution(mesh):
    placed = (P("seq", "head"), P("seq", "head"), P("seq", "head"), P(), P("head", None))
    return jax.shard_map(
        per_device, mesh=mesh, in_specs=placed, out_specs=P("seq", "head"), check_vma=False
    )
```

```python
import math

import jax
import jax.numpy as jnp
from jax import lax
from jax.experimental import pallas as pl
from jax.experimental.pallas import tpu as pltpu
from jax.sharding import PartitionSpec as P

HD = 64
BLOCK = 256
MASKED = -1e30
COST = 4


def flat_exchange(value, axis, mask):
    pairs = [(source, source ^ mask) for source in range(lax.axis_size(axis))]
    return lax.ppermute(value, axis, pairs)


def halo_exchange(value, axis):
    count = lax.axis_size(axis)
    pairs = []
    for source in range(count):
        target = source + 1 if source % 2 else source - 1
        if 0 <= target < count:
            pairs.append((source, target))
    return lax.ppermute(value, axis, pairs)


def after(value, *others):
    return lax.optimization_barrier((value, *others))[0]


def stacked_heads(q, heads):
    lane = lax.broadcasted_iota(jnp.int32, q.shape, 1)
    zero = jnp.zeros_like(q)
    return jnp.concatenate(
        [jnp.where((lane >= h * HD) & (lane < (h + 1) * HD), q, zero) for h in range(heads)], axis=0
    )


def fold(pieces, q, scores, scale, heads, m0, l0, acc0):
    qs = stacked_heads(q, heads)
    rows = qs.shape[0]
    half = rows // 2
    part = m0
    for at, (keys, _, bias) in enumerate(pieces):
        s = lax.dot_general(qs, keys(), (((1,), (1,)), ((), ())), preferred_element_type=jnp.float32)
        scores[at] = s
        top = jnp.maximum(s[:, :128], s[:, 128:]) + bias
        part = top if part is None else jnp.maximum(part, top)
    m = jnp.max(part, axis=1, keepdims=True)
    if l0 is None:
        total, acc_low, acc_high = None, None, None
    else:
        shrink = jnp.exp2((m0 - m) * scale)
        total = l0 * shrink
        acc_low = acc0[:half] * shrink[:half]
        acc_high = acc0[half:] * shrink[half:]
    for at, (_, values, bias) in enumerate(pieces):
        p = jnp.exp2((scores[at] - (m - bias)) * scale)
        add = p[:, :128] + p[:, 128:]
        total = add if total is None else total + add
        w = p.astype(jnp.bfloat16)
        v = values()
        low = jnp.dot(w[:half], v[:, :128], preferred_element_type=jnp.float32)
        high = jnp.dot(w[half:], v[:, 128:], preferred_element_type=jnp.float32)
        acc_low = low if acc_low is None else acc_low + low
        acc_high = high if acc_high is None else acc_high + high
    return m, total, jnp.concatenate([acc_low, acc_high], axis=0)


def bias_of(keep_ref, block, count):
    safe = jnp.clip(block, 0, count - 1)
    ok = (block >= 0) & (block < count) & (keep_ref[safe] == 1)
    return jnp.where(ok, 0.0, MASKED)


def part_of(ref, start):
    return (
        lambda: ref[pl.ds(start, BLOCK)],
        lambda: ref[pl.ds(pl.multiple_of(start + BLOCK, BLOCK), BLOCK)],
    )


def attend_kernel(scale, heads, local, plan, stateful, finish, rotated, keep_ref, q_ref, *refs):
    arrays = 1 + max(max(array) if isinstance(array, tuple) else array for _, array, _, _ in plan)
    sources, refs = refs[:arrays], refs[arrays:]
    m0, l0, acc0 = None, None, None
    if stateful:
        m0, l0, acc0 = (ref[...] for ref in refs[:3])
        refs = refs[3:]
    if finish:
        w_ref, *outs, scores, near = refs
        out_refs = outs if rotated else [outs[0].at[at] for at in range(outs[0].shape[0])]
    else:
        m_ref, l_ref, acc_ref, scores, near = refs
    count = keep_ref.shape[0]
    rank = lax.axis_index("seq")
    block = rank * 2 + local
    pieces = []
    for what, array, start, number in plan:
        if what == "near":
            core_ref, halo_ref = sources[array[0]], sources[array[1]]
            mine = lax.rem(rank, 2) == local

            @pl.when(mine)
            def _():
                near[...] = halo_ref[...]

            @pl.when(jnp.logical_not(mine))
            def _():
                near[...] = core_ref[start : start + 2 * BLOCK]

            pieces.append((*part_of(near, 0), bias_of(keep_ref, block + number, count)))
        elif what == "self":
            pieces.append((*part_of(sources[array], start), 0.0))
        else:
            pieces.append((*part_of(sources[array], start), bias_of(keep_ref, block ^ number, count)))
    q = q_ref[local * BLOCK : (local + 1) * BLOCK]
    m, total, acc = fold(pieces, q, scores, scale, heads, m0, l0, acc0)
    if not finish:
        m_ref[...] = jnp.broadcast_to(m, m_ref.shape)
        l_ref[...] = total
        acc_ref[...] = acc
        return
    mixed = acc / jnp.sum(total, axis=1, keepdims=True)
    lane = lax.broadcasted_iota(jnp.int32, (BLOCK, 128), 1)
    joined = []
    for pair in range(2):
        first = mixed[2 * pair * BLOCK : (2 * pair + 1) * BLOCK]
        second = mixed[(2 * pair + 1) * BLOCK : (2 * pair + 2) * BLOCK]
        joined.append(jnp.where(lane < HD, first, second))
    attended = jnp.concatenate(joined, axis=1).astype(jnp.bfloat16)
    groups = len(out_refs)
    columns = out_refs[0].shape[1]
    for group, out_ref in enumerate(out_refs):
        start = group * columns
        if rotated:
            start = pl.multiple_of(lax.rem(lax.axis_index("head") + group, groups) * columns, columns)
        w = w_ref[:, pl.ds(start, columns)]
        out_ref[...] = jnp.dot(attended, w, preferred_element_type=jnp.float32).astype(out_ref.dtype)


def attend(name, block_keep, queries, local, sources, plan, state=None, w_out=None, rotated=False):
    width = queries.shape[1]
    heads = width // HD
    stacked = heads * BLOCK
    scale = 1.0 / math.sqrt(HD) * math.log2(math.e)
    vmem = pl.BlockSpec(memory_space=pltpu.VMEM)
    smem = pl.BlockSpec(memory_space=pltpu.SMEM)
    finish = w_out is not None
    if finish:
        groups = lax.axis_size("head")
        columns = w_out.shape[1] // groups
        if rotated:
            shape = [jax.ShapeDtypeStruct((BLOCK, columns), jnp.bfloat16)] * groups
            specs = [vmem] * groups
        else:
            shape = jax.ShapeDtypeStruct((groups, BLOCK, columns), jnp.bfloat16)
            specs = vmem
    else:
        shape = [jax.ShapeDtypeStruct((stacked, 128), jnp.float32)] * 3
        specs = [vmem] * 3
    given = [block_keep, queries, *sources, *(state or ()), *((w_out,) if finish else ())]
    return pl.pallas_call(
        lambda *refs: attend_kernel(scale, heads, local, plan, state is not None, finish, rotated, *refs),
        out_shape=shape,
        in_specs=[smem] + [vmem] * (len(given) - 1),
        out_specs=specs,
        scratch_shapes=[
            pltpu.VMEM((len(plan), stacked, BLOCK), jnp.float32),
            pltpu.VMEM((2 * BLOCK, width), jnp.bfloat16),
        ],
        compiler_params=pltpu.CompilerParams(vmem_limit_bytes=(len(plan) + 7) << 20),
        cost_estimate=pl.CostEstimate(
            flops=len(plan) * 4 * stacked * BLOCK * width * COST,
            transcendentals=len(plan) * stacked * BLOCK,
            bytes_accessed=len(plan) * 2 * BLOCK * width * 2,
        ),
        name=name,
    )(*given)


def per_device(queries, keys, values, block_keep, w_out):
    parts = [
        jnp.concatenate([keys[at : at + BLOCK], values[at : at + BLOCK]], axis=0) for at in (0, BLOCK)
    ]
    packed = jnp.concatenate(parts, axis=0)
    side = lax.rem(lax.axis_index("seq"), 2)
    edge = jnp.where(side == 1, parts[1], parts[0])
    y4a = flat_exchange(parts[0], "seq", 1 << 3)
    y2 = flat_exchange(packed, "seq", 1 << 2)
    y1 = flat_exchange(packed, "seq", 1 << 1)
    core = flat_exchange(packed, "seq", 1)
    x1 = flat_exchange(after(packed, core), "seq", 1 << 4)
    x2 = flat_exchange(after(packed, core), "seq", 1 << 5)
    z1 = flat_exchange(after(packed, y1), "seq", 1 << 6)
    halo = halo_exchange(after(edge, x1), "seq")
    y4b = flat_exchange(after(parts[1], x1), "seq", 1 << 3)

    state0 = attend(
        "early0",
        block_keep,
        queries,
        0,
        [packed, core],
        [
            ("self", 0, 0, 0),
            ("xor", 0, 512, 1),
            ("xor", 1, 0, 2),
        ],
    )
    state1 = attend(
        "early1",
        block_keep,
        queries,
        1,
        [packed, core],
        [
            ("self", 0, 512, 0),
            ("xor", 0, 0, 1),
            ("xor", 1, 512, 2),
        ],
    )
    mine, *pieces = attend(
        "late0",
        block_keep,
        after(queries, state1[0]),
        0,
        [core, halo, z1, y1, y2, x1, x2, y4a],
        [
            ("near", (0, 1), 512, -1),
            ("xor", 2, 0, 128),
            ("xor", 3, 0, 4),
            ("xor", 4, 0, 8),
            ("xor", 5, 0, 32),
            ("xor", 6, 0, 64),
            ("xor", 7, 0, 16),
        ],
        state=state0,
        w_out=w_out,
        rotated=True,
    )
    groups = 1 + len(pieces)
    moved = [
        lax.ppermute(piece, "head", [(h, (h + hop + 1) % groups) for h in range(groups)])
        for hop, piece in enumerate(pieces)
    ]
    shares = attend(
        "late1",
        block_keep,
        after(queries, mine),
        1,
        [core, halo, z1, y1, y2, x1, x2, y4b],
        [
            ("near", (0, 1), 0, 1),
            ("xor", 2, 512, 128),
            ("xor", 3, 512, 4),
            ("xor", 4, 512, 8),
            ("xor", 5, 512, 32),
            ("xor", 6, 512, 64),
            ("xor", 7, 0, 16),
        ],
        state=state1,
        w_out=w_out,
    )
    spread = lax.all_to_all(after(shares, *moved), "head", 0, 0, tiled=False)
    total = mine.astype(jnp.float32)
    for piece in moved:
        total = total + piece.astype(jnp.float32)
    outs = [total, jnp.sum(spread.astype(jnp.float32), axis=0)]
    return jnp.concatenate([out.astype(jnp.bfloat16) for out in outs], axis=0)


def solution(mesh):
    placed = (P("seq", "head"), P("seq", "head"), P("seq", "head"), P(), P("head", None))
    return jax.shard_map(
        per_device, mesh=mesh, in_specs=placed, out_specs=P("seq", "head"), check_vma=False
    )
```

```python
import math

import jax
import jax.numpy as jnp
from jax import lax
from jax.experimental import pallas as pl
from jax.experimental.pallas import tpu as pltpu
from jax.sharding import PartitionSpec as P

HD = 64
BLOCK = 256
MASKED = -1e30
COST = 4


def flat_exchange(value, axis, mask):
    pairs = [(source, source ^ mask) for source in range(lax.axis_size(axis))]
    return lax.ppermute(value, axis, pairs)


def halo_exchange(value, axis):
    count = lax.axis_size(axis)
    pairs = []
    for source in range(count):
        target = source + 1 if source % 2 else source - 1
        if 0 <= target < count:
            pairs.append((source, target))
    return lax.ppermute(value, axis, pairs)


def after(value, *others):
    return lax.optimization_barrier((value, *others))[0]


def stacked_heads(q, heads):
    lane = lax.broadcasted_iota(jnp.int32, q.shape, 1)
    zero = jnp.zeros_like(q)
    return jnp.concatenate(
        [jnp.where((lane >= h * HD) & (lane < (h + 1) * HD), q, zero) for h in range(heads)], axis=0
    )


def fold(pieces, q, scores, scale, heads, m0, l0, acc0):
    qs = stacked_heads(q, heads)
    rows = qs.shape[0]
    half = rows // 2
    part = m0
    for at, (keys, _, bias) in enumerate(pieces):
        s = lax.dot_general(qs, keys(), (((1,), (1,)), ((), ())), preferred_element_type=jnp.float32)
        scores[at] = s
        top = jnp.maximum(s[:, :128], s[:, 128:]) + bias
        part = top if part is None else jnp.maximum(part, top)
    m = jnp.max(part, axis=1, keepdims=True)
    if l0 is None:
        total, acc_low, acc_high = None, None, None
    else:
        shrink = jnp.exp2((m0 - m) * scale)
        total = l0 * shrink
        acc_low = acc0[:half] * shrink[:half]
        acc_high = acc0[half:] * shrink[half:]
    for at, (_, values, bias) in enumerate(pieces):
        p = jnp.exp2((scores[at] - (m - bias)) * scale)
        add = p[:, :128] + p[:, 128:]
        total = add if total is None else total + add
        w = p.astype(jnp.bfloat16)
        v = values()
        low = jnp.dot(w[:half], v[:, :128], preferred_element_type=jnp.float32)
        high = jnp.dot(w[half:], v[:, 128:], preferred_element_type=jnp.float32)
        acc_low = low if acc_low is None else acc_low + low
        acc_high = high if acc_high is None else acc_high + high
    return m, total, jnp.concatenate([acc_low, acc_high], axis=0)


def bias_of(keep_ref, block, count):
    safe = jnp.clip(block, 0, count - 1)
    ok = (block >= 0) & (block < count) & (keep_ref[safe] == 1)
    return jnp.where(ok, 0.0, MASKED)


def part_of(ref, start):
    return (
        lambda: ref[pl.ds(start, BLOCK)],
        lambda: ref[pl.ds(pl.multiple_of(start + BLOCK, BLOCK), BLOCK)],
    )


def attend_kernel(scale, heads, local, plan, stateful, finish, rotated, keep_ref, q_ref, *refs):
    arrays = 1 + max(max(array) if isinstance(array, tuple) else array for _, array, _, _ in plan)
    sources, refs = refs[:arrays], refs[arrays:]
    m0, l0, acc0 = None, None, None
    if stateful:
        m0, l0, acc0 = (ref[...] for ref in refs[:3])
        refs = refs[3:]
    if finish:
        w_ref, *outs, scores, near = refs
        out_refs = outs if rotated else [outs[0].at[at] for at in range(outs[0].shape[0])]
    else:
        m_ref, l_ref, acc_ref, scores, near = refs
    count = keep_ref.shape[0]
    rank = lax.axis_index("seq")
    block = rank * 2 + local
    pieces = []
    for what, array, start, number in plan:
        if what == "near":
            core_ref, halo_ref = sources[array[0]], sources[array[1]]
            mine = lax.rem(rank, 2) == local

            @pl.when(mine)
            def _():
                near[...] = halo_ref[...]

            @pl.when(jnp.logical_not(mine))
            def _():
                near[...] = core_ref[start : start + 2 * BLOCK]

            pieces.append((*part_of(near, 0), bias_of(keep_ref, block + number, count)))
        elif what == "self":
            pieces.append((*part_of(sources[array], start), 0.0))
        else:
            pieces.append((*part_of(sources[array], start), bias_of(keep_ref, block ^ number, count)))
    q = q_ref[local * BLOCK : (local + 1) * BLOCK]
    m, total, acc = fold(pieces, q, scores, scale, heads, m0, l0, acc0)
    if not finish:
        m_ref[...] = jnp.broadcast_to(m, m_ref.shape)
        l_ref[...] = total
        acc_ref[...] = acc
        return
    mixed = acc / jnp.sum(total, axis=1, keepdims=True)
    lane = lax.broadcasted_iota(jnp.int32, (BLOCK, 128), 1)
    joined = []
    for pair in range(2):
        first = mixed[2 * pair * BLOCK : (2 * pair + 1) * BLOCK]
        second = mixed[(2 * pair + 1) * BLOCK : (2 * pair + 2) * BLOCK]
        joined.append(jnp.where(lane < HD, first, second))
    attended = jnp.concatenate(joined, axis=1).astype(jnp.bfloat16)
    groups = len(out_refs)
    columns = out_refs[0].shape[1]
    for group, out_ref in enumerate(out_refs):
        start = group * columns
        if rotated:
            start = pl.multiple_of(lax.rem(lax.axis_index("head") + group, groups) * columns, columns)
        w = w_ref[:, pl.ds(start, columns)]
        out_ref[...] = jnp.dot(attended, w, preferred_element_type=jnp.float32).astype(out_ref.dtype)


def attend(name, block_keep, queries, local, sources, plan, state=None, w_out=None, rotated=False):
    width = queries.shape[1]
    heads = width // HD
    stacked = heads * BLOCK
    scale = 1.0 / math.sqrt(HD) * math.log2(math.e)
    vmem = pl.BlockSpec(memory_space=pltpu.VMEM)
    smem = pl.BlockSpec(memory_space=pltpu.SMEM)
    finish = w_out is not None
    if finish:
        groups = lax.axis_size("head")
        columns = w_out.shape[1] // groups
        if rotated:
            shape = [jax.ShapeDtypeStruct((BLOCK, columns), jnp.bfloat16)] * groups
            specs = [vmem] * groups
        else:
            shape = jax.ShapeDtypeStruct((groups, BLOCK, columns), jnp.bfloat16)
            specs = vmem
    else:
        shape = [jax.ShapeDtypeStruct((stacked, 128), jnp.float32)] * 3
        specs = [vmem] * 3
    given = [block_keep, queries, *sources, *(state or ()), *((w_out,) if finish else ())]
    return pl.pallas_call(
        lambda *refs: attend_kernel(scale, heads, local, plan, state is not None, finish, rotated, *refs),
        out_shape=shape,
        in_specs=[smem] + [vmem] * (len(given) - 1),
        out_specs=specs,
        scratch_shapes=[
            pltpu.VMEM((len(plan), stacked, BLOCK), jnp.float32),
            pltpu.VMEM((2 * BLOCK, width), jnp.bfloat16),
        ],
        compiler_params=pltpu.CompilerParams(vmem_limit_bytes=(len(plan) + 7) << 20),
        cost_estimate=pl.CostEstimate(
            flops=len(plan) * 4 * stacked * BLOCK * width * COST,
            transcendentals=len(plan) * stacked * BLOCK,
            bytes_accessed=len(plan) * 2 * BLOCK * width * 2,
        ),
        name=name,
    )(*given)


def per_device(queries, keys, values, block_keep, w_out):
    parts = [
        jnp.concatenate([keys[at : at + BLOCK], values[at : at + BLOCK]], axis=0) for at in (0, BLOCK)
    ]
    packed = jnp.concatenate(parts, axis=0)
    side = lax.rem(lax.axis_index("seq"), 2)
    edge = jnp.where(side == 1, parts[1], parts[0])
    core = flat_exchange(packed, "seq", 1)
    halo = halo_exchange(edge, "seq")
    y4a = flat_exchange(parts[0], "seq", 1 << 3)
    y2 = flat_exchange(packed, "seq", 1 << 2)
    y1 = flat_exchange(packed, "seq", 1 << 1)
    x1 = flat_exchange(after(packed, core), "seq", 1 << 4)
    x2 = flat_exchange(after(packed, core), "seq", 1 << 5)
    z1 = flat_exchange(after(packed, y1), "seq", 1 << 6)
    y4b = flat_exchange(after(parts[1], x1), "seq", 1 << 3)

    state0 = attend(
        "early0",
        block_keep,
        queries,
        0,
        [packed, core, halo],
        [
            ("self", 0, 0, 0),
            ("xor", 0, 512, 1),
            ("xor", 1, 0, 2),
            ("near", (1, 2), 512, -1),
        ],
    )
    state1 = attend(
        "early1",
        block_keep,
        queries,
        1,
        [packed, core, halo],
        [
            ("self", 0, 512, 0),
            ("xor", 0, 0, 1),
            ("xor", 1, 512, 2),
            ("near", (1, 2), 0, 1),
        ],
    )
    mine, *pieces = attend(
        "late0",
        block_keep,
        after(queries, state1[0]),
        0,
        [z1, y1, y2, x1, x2, y4a],
        [
            ("xor", 0, 0, 128),
            ("xor", 1, 0, 4),
            ("xor", 2, 0, 8),
            ("xor", 3, 0, 32),
            ("xor", 4, 0, 64),
            ("xor", 5, 0, 16),
        ],
        state=state0,
        w_out=w_out,
        rotated=True,
    )
    groups = 1 + len(pieces)
    moved = [
        lax.ppermute(piece, "head", [(h, (h + hop + 1) % groups) for h in range(groups)])
        for hop, piece in enumerate(pieces)
    ]
    shares = attend(
        "late1",
        block_keep,
        after(queries, mine),
        1,
        [z1, y1, y2, x1, x2, y4b],
        [
            ("xor", 0, 512, 128),
            ("xor", 1, 512, 4),
            ("xor", 2, 512, 8),
            ("xor", 3, 512, 32),
            ("xor", 4, 512, 64),
            ("xor", 5, 0, 16),
        ],
        state=state1,
        w_out=w_out,
    )
    spread = lax.all_to_all(after(shares, *moved), "head", 0, 0, tiled=False)
    total = mine.astype(jnp.float32)
    for piece in moved:
        total = total + piece.astype(jnp.float32)
    outs = [total, jnp.sum(spread.astype(jnp.float32), axis=0)]
    return jnp.concatenate([out.astype(jnp.bfloat16) for out in outs], axis=0)


def solution(mesh):
    placed = (P("seq", "head"), P("seq", "head"), P("seq", "head"), P(), P("head", None))
    return jax.shard_map(
        per_device, mesh=mesh, in_specs=placed, out_specs=P("seq", "head"), check_vma=False
    )
```

```python
import math

import jax
import jax.numpy as jnp
from jax import lax
from jax.experimental import pallas as pl
from jax.experimental.pallas import tpu as pltpu
from jax.sharding import PartitionSpec as P

HD = 64
BLOCK = 256
MASKED = -1e30
COST = 4


def flat_exchange(value, axis, mask):
    pairs = [(source, source ^ mask) for source in range(lax.axis_size(axis))]
    return lax.ppermute(value, axis, pairs)


def halo_exchange(value, axis):
    count = lax.axis_size(axis)
    pairs = []
    for source in range(count):
        target = source + 1 if source % 2 else source - 1
        if 0 <= target < count:
            pairs.append((source, target))
    return lax.ppermute(value, axis, pairs)


def after(value, *others):
    return lax.optimization_barrier((value, *others))[0]


def stacked_heads(q, heads):
    lane = lax.broadcasted_iota(jnp.int32, q.shape, 1)
    zero = jnp.zeros_like(q)
    return jnp.concatenate(
        [jnp.where((lane >= h * HD) & (lane < (h + 1) * HD), q, zero) for h in range(heads)], axis=0
    )


def fold(pieces, q, scores, scale, heads, m0, l0, acc0):
    qs = stacked_heads(q, heads)
    rows = qs.shape[0]
    half = rows // 2
    part = m0
    for at, (keys, _, bias) in enumerate(pieces):
        s = lax.dot_general(qs, keys(), (((1,), (1,)), ((), ())), preferred_element_type=jnp.float32)
        scores[at] = s
        top = jnp.maximum(s[:, :128], s[:, 128:]) + bias
        part = top if part is None else jnp.maximum(part, top)
    m = jnp.max(part, axis=1, keepdims=True)
    if l0 is None:
        total, acc_low, acc_high = None, None, None
    else:
        shrink = jnp.exp2((m0 - m) * scale)
        total = l0 * shrink
        acc_low = acc0[:half] * shrink[:half]
        acc_high = acc0[half:] * shrink[half:]
    for at, (_, values, bias) in enumerate(pieces):
        p = jnp.exp2((scores[at] - (m - bias)) * scale)
        add = p[:, :128] + p[:, 128:]
        total = add if total is None else total + add
        w = p.astype(jnp.bfloat16)
        v = values()
        low = jnp.dot(w[:half], v[:, :128], preferred_element_type=jnp.float32)
        high = jnp.dot(w[half:], v[:, 128:], preferred_element_type=jnp.float32)
        acc_low = low if acc_low is None else acc_low + low
        acc_high = high if acc_high is None else acc_high + high
    return m, total, jnp.concatenate([acc_low, acc_high], axis=0)


def bias_of(keep_ref, block, count):
    safe = jnp.clip(block, 0, count - 1)
    ok = (block >= 0) & (block < count) & (keep_ref[safe] == 1)
    return jnp.where(ok, 0.0, MASKED)


def part_of(ref, start):
    return (
        lambda: ref[pl.ds(start, BLOCK)],
        lambda: ref[pl.ds(pl.multiple_of(start + BLOCK, BLOCK), BLOCK)],
    )


def attend_kernel(scale, heads, local, plan, stateful, finish, rotated, keep_ref, q_ref, *refs):
    arrays = 1 + max(max(array) if isinstance(array, tuple) else array for _, array, _, _ in plan)
    sources, refs = refs[:arrays], refs[arrays:]
    m0, l0, acc0 = None, None, None
    if stateful:
        m0, l0, acc0 = (ref[...] for ref in refs[:3])
        refs = refs[3:]
    if finish:
        w_ref, *outs, scores, near = refs
        out_refs = outs if rotated else [outs[0].at[at] for at in range(outs[0].shape[0])]
    else:
        m_ref, l_ref, acc_ref, scores, near = refs
    count = keep_ref.shape[0]
    rank = lax.axis_index("seq")
    block = rank * 2 + local
    pieces = []
    for what, array, start, number in plan:
        if what == "near":
            core_ref, halo_ref = sources[array[0]], sources[array[1]]
            mine = lax.rem(rank, 2) == local

            @pl.when(mine)
            def _():
                near[...] = halo_ref[...]

            @pl.when(jnp.logical_not(mine))
            def _():
                near[...] = core_ref[start : start + 2 * BLOCK]

            pieces.append((*part_of(near, 0), bias_of(keep_ref, block + number, count)))
        elif what == "self":
            pieces.append((*part_of(sources[array], start), 0.0))
        else:
            pieces.append((*part_of(sources[array], start), bias_of(keep_ref, block ^ number, count)))
    q = q_ref[local * BLOCK : (local + 1) * BLOCK]
    m, total, acc = fold(pieces, q, scores, scale, heads, m0, l0, acc0)
    if not finish:
        m_ref[...] = jnp.broadcast_to(m, m_ref.shape)
        l_ref[...] = total
        acc_ref[...] = acc
        return
    mixed = acc / jnp.sum(total, axis=1, keepdims=True)
    lane = lax.broadcasted_iota(jnp.int32, (BLOCK, 128), 1)
    joined = []
    for pair in range(2):
        first = mixed[2 * pair * BLOCK : (2 * pair + 1) * BLOCK]
        second = mixed[(2 * pair + 1) * BLOCK : (2 * pair + 2) * BLOCK]
        joined.append(jnp.where(lane < HD, first, second))
    attended = jnp.concatenate(joined, axis=1).astype(jnp.bfloat16)
    groups = len(out_refs)
    columns = out_refs[0].shape[1]
    for group, out_ref in enumerate(out_refs):
        start = group * columns
        if rotated:
            start = pl.multiple_of(lax.rem(lax.axis_index("head") + group, groups) * columns, columns)
        w = w_ref[:, pl.ds(start, columns)]
        out_ref[...] = jnp.dot(attended, w, preferred_element_type=jnp.float32).astype(out_ref.dtype)


def attend(name, block_keep, queries, local, sources, plan, state=None, w_out=None, rotated=False):
    width = queries.shape[1]
    heads = width // HD
    stacked = heads * BLOCK
    scale = 1.0 / math.sqrt(HD) * math.log2(math.e)
    vmem = pl.BlockSpec(memory_space=pltpu.VMEM)
    smem = pl.BlockSpec(memory_space=pltpu.SMEM)
    finish = w_out is not None
    if finish:
        groups = lax.axis_size("head")
        columns = w_out.shape[1] // groups
        if rotated:
            shape = [jax.ShapeDtypeStruct((BLOCK, columns), jnp.bfloat16)] * groups
            specs = [vmem] * groups
        else:
            shape = jax.ShapeDtypeStruct((groups, BLOCK, columns), jnp.bfloat16)
            specs = vmem
    else:
        shape = [jax.ShapeDtypeStruct((stacked, 128), jnp.float32)] * 3
        specs = [vmem] * 3
    given = [block_keep, queries, *sources, *(state or ()), *((w_out,) if finish else ())]
    return pl.pallas_call(
        lambda *refs: attend_kernel(scale, heads, local, plan, state is not None, finish, rotated, *refs),
        out_shape=shape,
        in_specs=[smem] + [vmem] * (len(given) - 1),
        out_specs=specs,
        scratch_shapes=[
            pltpu.VMEM((len(plan), stacked, BLOCK), jnp.float32),
            pltpu.VMEM((2 * BLOCK, width), jnp.bfloat16),
        ],
        compiler_params=pltpu.CompilerParams(vmem_limit_bytes=(len(plan) + 7) << 20),
        cost_estimate=pl.CostEstimate(
            flops=len(plan) * 4 * stacked * BLOCK * width * COST,
            transcendentals=len(plan) * stacked * BLOCK,
            bytes_accessed=len(plan) * 2 * BLOCK * width * 2,
        ),
        name=name,
    )(*given)


def per_device(queries, keys, values, block_keep, w_out):
    parts = [
        jnp.concatenate([keys[at : at + BLOCK], values[at : at + BLOCK]], axis=0) for at in (0, BLOCK)
    ]
    packed = jnp.concatenate(parts, axis=0)
    side = lax.rem(lax.axis_index("seq"), 2)
    edge = jnp.where(side == 1, parts[1], parts[0])
    core = flat_exchange(packed, "seq", 1)
    halo = halo_exchange(edge, "seq")
    y4a = flat_exchange(parts[0], "seq", 1 << 3)
    y2a = flat_exchange(parts[0], "seq", 1 << 2)
    y1 = flat_exchange(packed, "seq", 1 << 1)
    x1 = flat_exchange(after(packed, core), "seq", 1 << 4)
    x2 = flat_exchange(after(packed, x1), "seq", 1 << 5)
    z1 = flat_exchange(after(packed, x1), "seq", 1 << 6)
    y2b = flat_exchange(after(parts[1], y2a), "seq", 1 << 2)
    y4b = flat_exchange(after(parts[1], y2a), "seq", 1 << 3)

    state0 = attend(
        "early0",
        block_keep,
        queries,
        0,
        [packed, core, halo],
        [
            ("self", 0, 0, 0),
            ("xor", 0, 512, 1),
            ("xor", 1, 0, 2),
            ("near", (1, 2), 512, -1),
        ],
    )
    state1 = attend(
        "early1",
        block_keep,
        queries,
        1,
        [packed, core, halo],
        [
            ("self", 0, 512, 0),
            ("xor", 0, 0, 1),
            ("xor", 1, 512, 2),
            ("near", (1, 2), 0, 1),
        ],
    )
    mine, *pieces = attend(
        "late0",
        block_keep,
        after(queries, state1[0]),
        0,
        [z1, y1, x1, x2, y2a, y4a],
        [
            ("xor", 0, 0, 128),
            ("xor", 1, 0, 4),
            ("xor", 2, 0, 32),
            ("xor", 3, 0, 64),
            ("xor", 4, 0, 8),
            ("xor", 5, 0, 16),
        ],
        state=state0,
        w_out=w_out,
        rotated=True,
    )
    groups = 1 + len(pieces)
    moved = [
        lax.ppermute(piece, "head", [(h, (h + hop + 1) % groups) for h in range(groups)])
        for hop, piece in enumerate(pieces)
    ]
    shares = attend(
        "late1",
        block_keep,
        after(queries, mine),
        1,
        [z1, y1, x1, x2, y2b, y4b],
        [
            ("xor", 0, 512, 128),
            ("xor", 1, 512, 4),
            ("xor", 2, 512, 32),
            ("xor", 3, 512, 64),
            ("xor", 4, 0, 8),
            ("xor", 5, 0, 16),
        ],
        state=state1,
        w_out=w_out,
    )
    spread = lax.all_to_all(after(shares, *moved), "head", 0, 0, tiled=False)
    total = mine.astype(jnp.float32)
    for piece in moved:
        total = total + piece.astype(jnp.float32)
    outs = [total, jnp.sum(spread.astype(jnp.float32), axis=0)]
    return jnp.concatenate([out.astype(jnp.bfloat16) for out in outs], axis=0)


def solution(mesh):
    placed = (P("seq", "head"), P("seq", "head"), P("seq", "head"), P(), P("head", None))
    return jax.shard_map(
        per_device, mesh=mesh, in_specs=placed, out_specs=P("seq", "head"), check_vma=False
    )
```

```python
import math

import jax
import jax.numpy as jnp
from jax import lax
from jax.experimental import pallas as pl
from jax.experimental.pallas import tpu as pltpu
from jax.sharding import PartitionSpec as P

HD = 64
BLOCK = 256
MASKED = -1e30
COST = 4


def flat_exchange(value, axis, mask):
    pairs = [(source, source ^ mask) for source in range(lax.axis_size(axis))]
    return lax.ppermute(value, axis, pairs)


def halo_exchange(value, axis):
    count = lax.axis_size(axis)
    pairs = []
    for source in range(count):
        target = source + 1 if source % 2 else source - 1
        if 0 <= target < count:
            pairs.append((source, target))
    return lax.ppermute(value, axis, pairs)


def after(value, *others):
    return lax.optimization_barrier((value, *others))[0]


def stacked_heads(q, heads):
    lane = lax.broadcasted_iota(jnp.int32, q.shape, 1)
    zero = jnp.zeros_like(q)
    return jnp.concatenate(
        [jnp.where((lane >= h * HD) & (lane < (h + 1) * HD), q, zero) for h in range(heads)], axis=0
    )


def fold(pieces, q, scores, scale, heads, m0, l0, acc0):
    qs = stacked_heads(q, heads)
    rows = qs.shape[0]
    half = rows // 2
    part = m0
    for at, (keys, _, bias) in enumerate(pieces):
        s = lax.dot_general(qs, keys(), (((1,), (1,)), ((), ())), preferred_element_type=jnp.float32)
        scores[at] = s
        top = jnp.maximum(s[:, :128], s[:, 128:]) + bias
        part = top if part is None else jnp.maximum(part, top)
    m = jnp.max(part, axis=1, keepdims=True)
    if l0 is None:
        total, acc_low, acc_high = None, None, None
    else:
        shrink = jnp.exp2((m0 - m) * scale)
        total = l0 * shrink
        acc_low = acc0[:half] * shrink[:half]
        acc_high = acc0[half:] * shrink[half:]
    for at, (_, values, bias) in enumerate(pieces):
        p = jnp.exp2((scores[at] - (m - bias)) * scale)
        add = p[:, :128] + p[:, 128:]
        total = add if total is None else total + add
        w = p.astype(jnp.bfloat16)
        v = values()
        low = jnp.dot(w[:half], v[:, :128], preferred_element_type=jnp.float32)
        high = jnp.dot(w[half:], v[:, 128:], preferred_element_type=jnp.float32)
        acc_low = low if acc_low is None else acc_low + low
        acc_high = high if acc_high is None else acc_high + high
    return m, total, jnp.concatenate([acc_low, acc_high], axis=0)


def bias_of(keep_ref, block, count):
    safe = jnp.clip(block, 0, count - 1)
    ok = (block >= 0) & (block < count) & (keep_ref[safe] == 1)
    return jnp.where(ok, 0.0, MASKED)


def part_of(ref, start):
    return (
        lambda: ref[pl.ds(start, BLOCK)],
        lambda: ref[pl.ds(pl.multiple_of(start + BLOCK, BLOCK), BLOCK)],
    )


def attend_kernel(scale, heads, local, plan, stateful, finish, rotated, keep_ref, q_ref, *refs):
    arrays = 1 + max(max(array) if isinstance(array, tuple) else array for _, array, _, _ in plan)
    sources, refs = refs[:arrays], refs[arrays:]
    m0, l0, acc0 = None, None, None
    if stateful:
        m0, l0, acc0 = (ref[...] for ref in refs[:3])
        refs = refs[3:]
    if finish:
        w_ref, *outs, scores, near = refs
        out_refs = outs if rotated else [outs[0].at[at] for at in range(outs[0].shape[0])]
    else:
        m_ref, l_ref, acc_ref, scores, near = refs
    count = keep_ref.shape[0]
    rank = lax.axis_index("seq")
    block = rank * 2 + local
    pieces = []
    for what, array, start, number in plan:
        if what == "near":
            core_ref, halo_ref = sources[array[0]], sources[array[1]]
            mine = lax.rem(rank, 2) == local

            @pl.when(mine)
            def _():
                near[...] = halo_ref[...]

            @pl.when(jnp.logical_not(mine))
            def _():
                near[...] = core_ref[start : start + 2 * BLOCK]

            pieces.append((*part_of(near, 0), bias_of(keep_ref, block + number, count)))
        elif what == "self":
            pieces.append((*part_of(sources[array], start), 0.0))
        else:
            pieces.append((*part_of(sources[array], start), bias_of(keep_ref, block ^ number, count)))
    q = q_ref[local * BLOCK : (local + 1) * BLOCK]
    m, total, acc = fold(pieces, q, scores, scale, heads, m0, l0, acc0)
    if not finish:
        m_ref[...] = jnp.broadcast_to(m, m_ref.shape)
        l_ref[...] = total
        acc_ref[...] = acc
        return
    mixed = acc / jnp.sum(total, axis=1, keepdims=True)
    lane = lax.broadcasted_iota(jnp.int32, (BLOCK, 128), 1)
    joined = []
    for pair in range(2):
        first = mixed[2 * pair * BLOCK : (2 * pair + 1) * BLOCK]
        second = mixed[(2 * pair + 1) * BLOCK : (2 * pair + 2) * BLOCK]
        joined.append(jnp.where(lane < HD, first, second))
    attended = jnp.concatenate(joined, axis=1).astype(jnp.bfloat16)
    groups = len(out_refs)
    columns = out_refs[0].shape[1]
    for group, out_ref in enumerate(out_refs):
        start = group * columns
        if rotated:
            start = pl.multiple_of(lax.rem(lax.axis_index("head") + group, groups) * columns, columns)
        w = w_ref[:, pl.ds(start, columns)]
        out_ref[...] = jnp.dot(attended, w, preferred_element_type=jnp.float32).astype(out_ref.dtype)


def attend(name, block_keep, queries, local, sources, plan, state=None, w_out=None, rotated=False):
    width = queries.shape[1]
    heads = width // HD
    stacked = heads * BLOCK
    scale = 1.0 / math.sqrt(HD) * math.log2(math.e)
    vmem = pl.BlockSpec(memory_space=pltpu.VMEM)
    smem = pl.BlockSpec(memory_space=pltpu.SMEM)
    finish = w_out is not None
    if finish:
        groups = lax.axis_size("head")
        columns = w_out.shape[1] // groups
        if rotated:
            shape = [jax.ShapeDtypeStruct((BLOCK, columns), jnp.bfloat16)] * groups
            specs = [vmem] * groups
        else:
            shape = jax.ShapeDtypeStruct((groups, BLOCK, columns), jnp.bfloat16)
            specs = vmem
    else:
        shape = [jax.ShapeDtypeStruct((stacked, 128), jnp.float32)] * 3
        specs = [vmem] * 3
    given = [block_keep, queries, *sources, *(state or ()), *((w_out,) if finish else ())]
    return pl.pallas_call(
        lambda *refs: attend_kernel(scale, heads, local, plan, state is not None, finish, rotated, *refs),
        out_shape=shape,
        in_specs=[smem] + [vmem] * (len(given) - 1),
        out_specs=specs,
        scratch_shapes=[
            pltpu.VMEM((len(plan), stacked, BLOCK), jnp.float32),
            pltpu.VMEM((2 * BLOCK, width), jnp.bfloat16),
        ],
        compiler_params=pltpu.CompilerParams(vmem_limit_bytes=(len(plan) + 7) << 20),
        cost_estimate=pl.CostEstimate(
            flops=len(plan) * 4 * stacked * BLOCK * width * COST,
            transcendentals=len(plan) * stacked * BLOCK,
            bytes_accessed=len(plan) * 2 * BLOCK * width * 2,
        ),
        name=name,
    )(*given)


def per_device(queries, keys, values, block_keep, w_out):
    parts = [
        jnp.concatenate([keys[at : at + BLOCK], values[at : at + BLOCK]], axis=0) for at in (0, BLOCK)
    ]
    packed = jnp.concatenate(parts, axis=0)
    side = lax.rem(lax.axis_index("seq"), 2)
    edge = jnp.where(side == 1, parts[1], parts[0])
    core = flat_exchange(packed, "seq", 1)
    halo = halo_exchange(edge, "seq")
    y4a = flat_exchange(parts[0], "seq", 1 << 3)
    y2a = flat_exchange(parts[0], "seq", 1 << 2)
    y1 = flat_exchange(packed, "seq", 1 << 1)
    x1 = flat_exchange(after(packed, core), "seq", 1 << 4)
    x2 = flat_exchange(after(packed, halo), "seq", 1 << 5)
    z1 = flat_exchange(after(packed, y1), "seq", 1 << 6)
    y2b = flat_exchange(after(parts[1], x1), "seq", 1 << 2)
    y4b = flat_exchange(after(parts[1], x1), "seq", 1 << 3)

    state0 = attend(
        "early0",
        block_keep,
        queries,
        0,
        [packed, core, halo],
        [
            ("self", 0, 0, 0),
            ("xor", 0, 512, 1),
            ("xor", 1, 0, 2),
            ("near", (1, 2), 512, -1),
        ],
    )
    state1 = attend(
        "early1",
        block_keep,
        queries,
        1,
        [packed, core, halo],
        [
            ("self", 0, 512, 0),
            ("xor", 0, 0, 1),
            ("xor", 1, 512, 2),
            ("near", (1, 2), 0, 1),
        ],
    )
    mine, *pieces = attend(
        "late0",
        block_keep,
        after(queries, state1[0]),
        0,
        [z1, y1, x1, x2, y2a, y4a],
        [
            ("xor", 0, 0, 128),
            ("xor", 1, 0, 4),
            ("xor", 2, 0, 32),
            ("xor", 3, 0, 64),
            ("xor", 4, 0, 8),
            ("xor", 5, 0, 16),
        ],
        state=state0,
        w_out=w_out,
        rotated=True,
    )
    groups = 1 + len(pieces)
    moved = [
        lax.ppermute(piece, "head", [(h, (h + hop + 1) % groups) for h in range(groups)])
        for hop, piece in enumerate(pieces)
    ]
    shares = attend(
        "late1",
        block_keep,
        after(queries, mine),
        1,
        [z1, y1, x1, x2, y2b, y4b],
        [
            ("xor", 0, 512, 128),
            ("xor", 1, 512, 4),
            ("xor", 2, 512, 32),
            ("xor", 3, 512, 64),
            ("xor", 4, 0, 8),
            ("xor", 5, 0, 16),
        ],
        state=state1,
        w_out=w_out,
    )
    spread = lax.all_to_all(after(shares, *moved), "head", 0, 0, tiled=False)
    total = mine.astype(jnp.float32)
    for piece in moved:
        total = total + piece.astype(jnp.float32)
    outs = [total, jnp.sum(spread.astype(jnp.float32), axis=0)]
    return jnp.concatenate([out.astype(jnp.bfloat16) for out in outs], axis=0)


def solution(mesh):
    placed = (P("seq", "head"), P("seq", "head"), P("seq", "head"), P(), P("head", None))
    return jax.shard_map(
        per_device, mesh=mesh, in_specs=placed, out_specs=P("seq", "head"), check_vma=False
    )
```

```python
import math

import jax
import jax.numpy as jnp
from jax import lax
from jax.experimental import pallas as pl
from jax.experimental.pallas import tpu as pltpu
from jax.sharding import PartitionSpec as P

HD = 64
BLOCK = 256
MASKED = -1e30
COST = 4


def flat_exchange(value, axis, mask):
    pairs = [(source, source ^ mask) for source in range(lax.axis_size(axis))]
    return lax.ppermute(value, axis, pairs)


def halo_exchange(value, axis):
    count = lax.axis_size(axis)
    pairs = []
    for source in range(count):
        target = source + 1 if source % 2 else source - 1
        if 0 <= target < count:
            pairs.append((source, target))
    return lax.ppermute(value, axis, pairs)


def after(value, *others):
    return lax.optimization_barrier((value, *others))[0]


def stacked_heads(q, heads):
    lane = lax.broadcasted_iota(jnp.int32, q.shape, 1)
    zero = jnp.zeros_like(q)
    return jnp.concatenate(
        [jnp.where((lane >= h * HD) & (lane < (h + 1) * HD), q, zero) for h in range(heads)], axis=0
    )


def fold(pieces, q, scores, scale, heads, m0, l0, acc0):
    qs = stacked_heads(q, heads)
    rows = qs.shape[0]
    half = rows // 2
    part = m0
    for at, (keys, _, bias) in enumerate(pieces):
        s = lax.dot_general(qs, keys(), (((1,), (1,)), ((), ())), preferred_element_type=jnp.float32)
        scores[at] = s
        top = jnp.maximum(s[:, :128], s[:, 128:]) + bias
        part = top if part is None else jnp.maximum(part, top)
    m = jnp.max(part, axis=1, keepdims=True)
    if l0 is None:
        total, acc_low, acc_high = None, None, None
    else:
        shrink = jnp.exp2((m0 - m) * scale)
        total = l0 * shrink
        acc_low = acc0[:half] * shrink[:half]
        acc_high = acc0[half:] * shrink[half:]
    for at, (_, values, bias) in enumerate(pieces):
        p = jnp.exp2((scores[at] - (m - bias)) * scale)
        add = p[:, :128] + p[:, 128:]
        total = add if total is None else total + add
        w = p.astype(jnp.bfloat16)
        v = values()
        low = jnp.dot(w[:half], v[:, :128], preferred_element_type=jnp.float32)
        high = jnp.dot(w[half:], v[:, 128:], preferred_element_type=jnp.float32)
        acc_low = low if acc_low is None else acc_low + low
        acc_high = high if acc_high is None else acc_high + high
    return m, total, jnp.concatenate([acc_low, acc_high], axis=0)


def bias_of(keep_ref, block, count):
    safe = jnp.clip(block, 0, count - 1)
    ok = (block >= 0) & (block < count) & (keep_ref[safe] == 1)
    return jnp.where(ok, 0.0, MASKED)


def part_of(ref, start):
    return (
        lambda: ref[pl.ds(start, BLOCK)],
        lambda: ref[pl.ds(pl.multiple_of(start + BLOCK, BLOCK), BLOCK)],
    )


def attend_kernel(scale, heads, local, plan, stateful, finish, rotated, keep_ref, q_ref, *refs):
    arrays = 1 + max(max(array) if isinstance(array, tuple) else array for _, array, _, _ in plan)
    sources, refs = refs[:arrays], refs[arrays:]
    m0, l0, acc0 = None, None, None
    if stateful:
        m0, l0, acc0 = (ref[...] for ref in refs[:3])
        refs = refs[3:]
    if finish:
        w_ref, *outs, scores, near = refs
        out_refs = outs if rotated else [outs[0].at[at] for at in range(outs[0].shape[0])]
    else:
        m_ref, l_ref, acc_ref, scores, near = refs
    count = keep_ref.shape[0]
    rank = lax.axis_index("seq")
    block = rank * 2 + local
    pieces = []
    for what, array, start, number in plan:
        if what == "near":
            core_ref, halo_ref = sources[array[0]], sources[array[1]]
            mine = lax.rem(rank, 2) == local

            @pl.when(mine)
            def _():
                near[...] = halo_ref[...]

            @pl.when(jnp.logical_not(mine))
            def _():
                near[...] = core_ref[start : start + 2 * BLOCK]

            pieces.append((*part_of(near, 0), bias_of(keep_ref, block + number, count)))
        elif what == "self":
            pieces.append((*part_of(sources[array], start), 0.0))
        else:
            pieces.append((*part_of(sources[array], start), bias_of(keep_ref, block ^ number, count)))
    q = q_ref[local * BLOCK : (local + 1) * BLOCK]
    m, total, acc = fold(pieces, q, scores, scale, heads, m0, l0, acc0)
    if not finish:
        m_ref[...] = jnp.broadcast_to(m, m_ref.shape)
        l_ref[...] = total
        acc_ref[...] = acc
        return
    mixed = acc / jnp.sum(total, axis=1, keepdims=True)
    lane = lax.broadcasted_iota(jnp.int32, (BLOCK, 128), 1)
    joined = []
    for pair in range(2):
        first = mixed[2 * pair * BLOCK : (2 * pair + 1) * BLOCK]
        second = mixed[(2 * pair + 1) * BLOCK : (2 * pair + 2) * BLOCK]
        joined.append(jnp.where(lane < HD, first, second))
    attended = jnp.concatenate(joined, axis=1).astype(jnp.bfloat16)
    groups = len(out_refs)
    columns = out_refs[0].shape[1]
    for group, out_ref in enumerate(out_refs):
        start = group * columns
        if rotated:
            start = pl.multiple_of(lax.rem(lax.axis_index("head") + group, groups) * columns, columns)
        w = w_ref[:, pl.ds(start, columns)]
        out_ref[...] = jnp.dot(attended, w, preferred_element_type=jnp.float32).astype(out_ref.dtype)


def attend(name, block_keep, queries, local, sources, plan, state=None, w_out=None, rotated=False):
    width = queries.shape[1]
    heads = width // HD
    stacked = heads * BLOCK
    scale = 1.0 / math.sqrt(HD) * math.log2(math.e)
    vmem = pl.BlockSpec(memory_space=pltpu.VMEM)
    smem = pl.BlockSpec(memory_space=pltpu.SMEM)
    finish = w_out is not None
    if finish:
        groups = lax.axis_size("head")
        columns = w_out.shape[1] // groups
        if rotated:
            shape = [jax.ShapeDtypeStruct((BLOCK, columns), jnp.bfloat16)] * groups
            specs = [vmem] * groups
        else:
            shape = jax.ShapeDtypeStruct((groups, BLOCK, columns), jnp.bfloat16)
            specs = vmem
    else:
        shape = [jax.ShapeDtypeStruct((stacked, 128), jnp.float32)] * 3
        specs = [vmem] * 3
    given = [block_keep, queries, *sources, *(state or ()), *((w_out,) if finish else ())]
    return pl.pallas_call(
        lambda *refs: attend_kernel(scale, heads, local, plan, state is not None, finish, rotated, *refs),
        out_shape=shape,
        in_specs=[smem] + [vmem] * (len(given) - 1),
        out_specs=specs,
        scratch_shapes=[
            pltpu.VMEM((len(plan), stacked, BLOCK), jnp.float32),
            pltpu.VMEM((2 * BLOCK, width), jnp.bfloat16),
        ],
        compiler_params=pltpu.CompilerParams(vmem_limit_bytes=(len(plan) + 7) << 20),
        cost_estimate=pl.CostEstimate(
            flops=len(plan) * 4 * stacked * BLOCK * width * COST,
            transcendentals=len(plan) * stacked * BLOCK,
            bytes_accessed=len(plan) * 2 * BLOCK * width * 2,
        ),
        name=name,
    )(*given)


def per_device(queries, keys, values, block_keep, w_out):
    parts = [
        jnp.concatenate([keys[at : at + BLOCK], values[at : at + BLOCK]], axis=0) for at in (0, BLOCK)
    ]
    packed = jnp.concatenate(parts, axis=0)
    side = lax.rem(lax.axis_index("seq"), 2)
    edge = jnp.where(side == 1, parts[1], parts[0])
    core = flat_exchange(packed, "seq", 1)
    halo = halo_exchange(edge, "seq")
    y4a = flat_exchange(parts[0], "seq", 1 << 3)
    y2a = flat_exchange(parts[0], "seq", 1 << 2)
    y1 = flat_exchange(after(packed, halo), "seq", 1 << 1)
    x1 = flat_exchange(after(packed, core), "seq", 1 << 4)
    x2 = flat_exchange(after(packed, halo), "seq", 1 << 5)
    z1 = flat_exchange(after(packed, y1), "seq", 1 << 6)
    y2b = flat_exchange(after(parts[1], x1), "seq", 1 << 2)
    y4b = flat_exchange(after(parts[1], x1), "seq", 1 << 3)

    state0 = attend(
        "early0",
        block_keep,
        queries,
        0,
        [packed, core, halo],
        [
            ("self", 0, 0, 0),
            ("xor", 0, 512, 1),
            ("xor", 1, 0, 2),
            ("near", (1, 2), 512, -1),
        ],
    )
    state1 = attend(
        "early1",
        block_keep,
        queries,
        1,
        [packed, core, halo],
        [
            ("self", 0, 512, 0),
            ("xor", 0, 0, 1),
            ("xor", 1, 512, 2),
            ("near", (1, 2), 0, 1),
        ],
    )
    mine, *pieces = attend(
        "late0",
        block_keep,
        after(queries, state1[0]),
        0,
        [z1, y1, x1, x2, y2a, y4a],
        [
            ("xor", 0, 0, 128),
            ("xor", 1, 0, 4),
            ("xor", 2, 0, 32),
            ("xor", 3, 0, 64),
            ("xor", 4, 0, 8),
            ("xor", 5, 0, 16),
        ],
        state=state0,
        w_out=w_out,
        rotated=True,
    )
    groups = 1 + len(pieces)
    moved = [
        lax.ppermute(piece, "head", [(h, (h + hop + 1) % groups) for h in range(groups)])
        for hop, piece in enumerate(pieces)
    ]
    shares = attend(
        "late1",
        block_keep,
        after(queries, mine),
        1,
        [z1, y1, x1, x2, y2b, y4b],
        [
            ("xor", 0, 512, 128),
            ("xor", 1, 512, 4),
            ("xor", 2, 512, 32),
            ("xor", 3, 512, 64),
            ("xor", 4, 0, 8),
            ("xor", 5, 0, 16),
        ],
        state=state1,
        w_out=w_out,
    )
    spread = lax.all_to_all(after(shares, *moved), "head", 0, 0, tiled=False)
    total = mine.astype(jnp.float32)
    for piece in moved:
        total = total + piece.astype(jnp.float32)
    outs = [total, jnp.sum(spread.astype(jnp.float32), axis=0)]
    return jnp.concatenate([out.astype(jnp.bfloat16) for out in outs], axis=0)


def solution(mesh):
    placed = (P("seq", "head"), P("seq", "head"), P("seq", "head"), P(), P("head", None))
    return jax.shard_map(
        per_device, mesh=mesh, in_specs=placed, out_specs=P("seq", "head"), check_vma=False
    )
```

```python
import math

import jax
import jax.numpy as jnp
from jax import lax
from jax.experimental import pallas as pl
from jax.experimental.pallas import tpu as pltpu
from jax.sharding import PartitionSpec as P

HD = 64
BLOCK = 256
MASKED = -1e30
COST = 4


def flat_exchange(value, axis, mask):
    pairs = [(source, source ^ mask) for source in range(lax.axis_size(axis))]
    return lax.ppermute(value, axis, pairs)


def halo_exchange(value, axis):
    count = lax.axis_size(axis)
    pairs = []
    for source in range(count):
        target = source + 1 if source % 2 else source - 1
        if 0 <= target < count:
            pairs.append((source, target))
    return lax.ppermute(value, axis, pairs)


def after(value, *others):
    return lax.optimization_barrier((value, *others))[0]


def stacked_heads(q, heads):
    lane = lax.broadcasted_iota(jnp.int32, q.shape, 1)
    zero = jnp.zeros_like(q)
    return jnp.concatenate(
        [jnp.where((lane >= h * HD) & (lane < (h + 1) * HD), q, zero) for h in range(heads)], axis=0
    )


def fold(pieces, q, scores, scale, heads, m0, l0, acc0):
    qs = stacked_heads(q, heads)
    rows = qs.shape[0]
    half = rows // 2
    part = m0
    for at, (keys, _, bias) in enumerate(pieces):
        s = lax.dot_general(qs, keys(), (((1,), (1,)), ((), ())), preferred_element_type=jnp.float32)
        scores[at] = s
        top = jnp.maximum(s[:, :128], s[:, 128:]) + bias
        part = top if part is None else jnp.maximum(part, top)
    m = jnp.max(part, axis=1, keepdims=True)
    if l0 is None:
        total, acc_low, acc_high = None, None, None
    else:
        shrink = jnp.exp2((m0 - m) * scale)
        total = l0 * shrink
        acc_low = acc0[:half] * shrink[:half]
        acc_high = acc0[half:] * shrink[half:]
    for at, (_, values, bias) in enumerate(pieces):
        p = jnp.exp2((scores[at] - (m - bias)) * scale)
        add = p[:, :128] + p[:, 128:]
        total = add if total is None else total + add
        w = p.astype(jnp.bfloat16)
        v = values()
        low = jnp.dot(w[:half], v[:, :128], preferred_element_type=jnp.float32)
        high = jnp.dot(w[half:], v[:, 128:], preferred_element_type=jnp.float32)
        acc_low = low if acc_low is None else acc_low + low
        acc_high = high if acc_high is None else acc_high + high
    return m, total, jnp.concatenate([acc_low, acc_high], axis=0)


def bias_of(keep_ref, block, count):
    safe = jnp.clip(block, 0, count - 1)
    ok = (block >= 0) & (block < count) & (keep_ref[safe] == 1)
    return jnp.where(ok, 0.0, MASKED)


def part_of(ref, start):
    return (
        lambda: ref[pl.ds(start, BLOCK)],
        lambda: ref[pl.ds(pl.multiple_of(start + BLOCK, BLOCK), BLOCK)],
    )


def attend_kernel(scale, heads, local, plan, stateful, finish, rotated, keep_ref, q_ref, *refs):
    arrays = 1 + max(max(array) if isinstance(array, tuple) else array for _, array, _, _ in plan)
    sources, refs = refs[:arrays], refs[arrays:]
    m0, l0, acc0 = None, None, None
    if stateful:
        m0, l0, acc0 = (ref[...] for ref in refs[:3])
        refs = refs[3:]
    if finish:
        w_ref, *outs, scores, near = refs
        out_refs = outs if rotated else [outs[0].at[at] for at in range(outs[0].shape[0])]
    else:
        m_ref, l_ref, acc_ref, scores, near = refs
    count = keep_ref.shape[0]
    rank = lax.axis_index("seq")
    block = rank * 2 + local
    pieces = []
    for what, array, start, number in plan:
        if what == "near":
            core_ref, halo_ref = sources[array[0]], sources[array[1]]
            mine = lax.rem(rank, 2) == local

            @pl.when(mine)
            def _():
                near[...] = halo_ref[...]

            @pl.when(jnp.logical_not(mine))
            def _():
                near[...] = core_ref[start : start + 2 * BLOCK]

            pieces.append((*part_of(near, 0), bias_of(keep_ref, block + number, count)))
        elif what == "self":
            pieces.append((*part_of(sources[array], start), 0.0))
        else:
            pieces.append((*part_of(sources[array], start), bias_of(keep_ref, block ^ number, count)))
    q = q_ref[local * BLOCK : (local + 1) * BLOCK]
    m, total, acc = fold(pieces, q, scores, scale, heads, m0, l0, acc0)
    if not finish:
        m_ref[...] = jnp.broadcast_to(m, m_ref.shape)
        l_ref[...] = total
        acc_ref[...] = acc
        return
    mixed = acc / jnp.sum(total, axis=1, keepdims=True)
    lane = lax.broadcasted_iota(jnp.int32, (BLOCK, 128), 1)
    joined = []
    for pair in range(2):
        first = mixed[2 * pair * BLOCK : (2 * pair + 1) * BLOCK]
        second = mixed[(2 * pair + 1) * BLOCK : (2 * pair + 2) * BLOCK]
        joined.append(jnp.where(lane < HD, first, second))
    attended = jnp.concatenate(joined, axis=1).astype(jnp.bfloat16)
    groups = len(out_refs)
    columns = out_refs[0].shape[1]
    for group, out_ref in enumerate(out_refs):
        start = group * columns
        if rotated:
            start = pl.multiple_of(lax.rem(lax.axis_index("head") + group, groups) * columns, columns)
        w = w_ref[:, pl.ds(start, columns)]
        out_ref[...] = jnp.dot(attended, w, preferred_element_type=jnp.float32).astype(out_ref.dtype)


def attend(name, block_keep, queries, local, sources, plan, state=None, w_out=None, rotated=False):
    width = queries.shape[1]
    heads = width // HD
    stacked = heads * BLOCK
    scale = 1.0 / math.sqrt(HD) * math.log2(math.e)
    vmem = pl.BlockSpec(memory_space=pltpu.VMEM)
    smem = pl.BlockSpec(memory_space=pltpu.SMEM)
    finish = w_out is not None
    if finish:
        groups = lax.axis_size("head")
        columns = w_out.shape[1] // groups
        if rotated:
            shape = [jax.ShapeDtypeStruct((BLOCK, columns), jnp.bfloat16)] * groups
            specs = [vmem] * groups
        else:
            shape = jax.ShapeDtypeStruct((groups, BLOCK, columns), jnp.bfloat16)
            specs = vmem
    else:
        shape = [jax.ShapeDtypeStruct((stacked, 128), jnp.float32)] * 3
        specs = [vmem] * 3
    given = [block_keep, queries, *sources, *(state or ()), *((w_out,) if finish else ())]
    return pl.pallas_call(
        lambda *refs: attend_kernel(scale, heads, local, plan, state is not None, finish, rotated, *refs),
        out_shape=shape,
        in_specs=[smem] + [vmem] * (len(given) - 1),
        out_specs=specs,
        scratch_shapes=[
            pltpu.VMEM((len(plan), stacked, BLOCK), jnp.float32),
            pltpu.VMEM((2 * BLOCK, width), jnp.bfloat16),
        ],
        compiler_params=pltpu.CompilerParams(vmem_limit_bytes=(len(plan) + 7) << 20),
        cost_estimate=pl.CostEstimate(
            flops=len(plan) * 4 * stacked * BLOCK * width * COST,
            transcendentals=len(plan) * stacked * BLOCK,
            bytes_accessed=len(plan) * 2 * BLOCK * width * 2,
        ),
        name=name,
    )(*given)


def per_device(queries, keys, values, block_keep, w_out):
    parts = [
        jnp.concatenate([keys[at : at + BLOCK], values[at : at + BLOCK]], axis=0) for at in (0, BLOCK)
    ]
    packed = jnp.concatenate(parts, axis=0)
    side = lax.rem(lax.axis_index("seq"), 2)
    edge = jnp.where(side == 1, parts[1], parts[0])
    core = flat_exchange(packed, "seq", 1)
    halo = halo_exchange(edge, "seq")
    y4a = flat_exchange(parts[0], "seq", 1 << 3)
    y2a = flat_exchange(parts[0], "seq", 1 << 2)
    y1 = flat_exchange(after(packed, halo), "seq", 1 << 1)
    x1 = flat_exchange(after(packed, halo), "seq", 1 << 4)
    x2 = flat_exchange(after(packed, halo), "seq", 1 << 5)
    z1 = flat_exchange(after(packed, y1), "seq", 1 << 6)
    y2b = flat_exchange(after(parts[1], y1), "seq", 1 << 2)
    y4b = flat_exchange(after(parts[1], y1), "seq", 1 << 3)

    state0 = attend(
        "early0",
        block_keep,
        queries,
        0,
        [packed, core, halo],
        [
            ("self", 0, 0, 0),
            ("xor", 0, 512, 1),
            ("xor", 1, 0, 2),
            ("near", (1, 2), 512, -1),
        ],
    )
    state1 = attend(
        "early1",
        block_keep,
        queries,
        1,
        [packed, core, halo],
        [
            ("self", 0, 512, 0),
            ("xor", 0, 0, 1),
            ("xor", 1, 512, 2),
            ("near", (1, 2), 0, 1),
        ],
    )
    mine, *pieces = attend(
        "late0",
        block_keep,
        after(queries, state1[0]),
        0,
        [z1, y1, x1, x2, y2a, y4a],
        [
            ("xor", 0, 0, 128),
            ("xor", 1, 0, 4),
            ("xor", 2, 0, 32),
            ("xor", 3, 0, 64),
            ("xor", 4, 0, 8),
            ("xor", 5, 0, 16),
        ],
        state=state0,
        w_out=w_out,
        rotated=True,
    )
    groups = 1 + len(pieces)
    moved = [
        lax.ppermute(piece, "head", [(h, (h + hop + 1) % groups) for h in range(groups)])
        for hop, piece in enumerate(pieces)
    ]
    shares = attend(
        "late1",
        block_keep,
        after(queries, mine),
        1,
        [z1, y1, x1, x2, y2b, y4b],
        [
            ("xor", 0, 512, 128),
            ("xor", 1, 512, 4),
            ("xor", 2, 512, 32),
            ("xor", 3, 512, 64),
            ("xor", 4, 0, 8),
            ("xor", 5, 0, 16),
        ],
        state=state1,
        w_out=w_out,
    )
    spread = lax.all_to_all(after(shares, *moved), "head", 0, 0, tiled=False)
    total = mine.astype(jnp.float32)
    for piece in moved:
        total = total + piece.astype(jnp.float32)
    outs = [total, jnp.sum(spread.astype(jnp.float32), axis=0)]
    return jnp.concatenate([out.astype(jnp.bfloat16) for out in outs], axis=0)


def solution(mesh):
    placed = (P("seq", "head"), P("seq", "head"), P("seq", "head"), P(), P("head", None))
    return jax.shard_map(
        per_device, mesh=mesh, in_specs=placed, out_specs=P("seq", "head"), check_vma=False
    )
```

```python
import math

import jax
import jax.numpy as jnp
from jax import lax
from jax.experimental import pallas as pl
from jax.experimental.pallas import tpu as pltpu
from jax.sharding import PartitionSpec as P

HD = 64
BLOCK = 256
MASKED = -1e30
COST = 4


def flat_exchange(value, axis, mask):
    pairs = [(source, source ^ mask) for source in range(lax.axis_size(axis))]
    return lax.ppermute(value, axis, pairs)


def halo_exchange(value, axis):
    count = lax.axis_size(axis)
    pairs = []
    for source in range(count):
        target = source + 1 if source % 2 else source - 1
        if 0 <= target < count:
            pairs.append((source, target))
    return lax.ppermute(value, axis, pairs)


def after(value, *others):
    return lax.optimization_barrier((value, *others))[0]


def stacked_heads(q, heads):
    lane = lax.broadcasted_iota(jnp.int32, q.shape, 1)
    zero = jnp.zeros_like(q)
    return jnp.concatenate(
        [jnp.where((lane >= h * HD) & (lane < (h + 1) * HD), q, zero) for h in range(heads)], axis=0
    )


def fold(pieces, q, scores, scale, heads, m0, l0, acc0):
    qs = stacked_heads(q, heads)
    rows = qs.shape[0]
    half = rows // 2
    part = m0
    for at, (keys, _, bias) in enumerate(pieces):
        s = lax.dot_general(qs, keys(), (((1,), (1,)), ((), ())), preferred_element_type=jnp.float32)
        scores[at] = s
        top = jnp.maximum(s[:, :128], s[:, 128:]) + bias
        part = top if part is None else jnp.maximum(part, top)
    m = jnp.max(part, axis=1, keepdims=True)
    if l0 is None:
        total, acc_low, acc_high = None, None, None
    else:
        shrink = jnp.exp2((m0 - m) * scale)
        total = l0 * shrink
        acc_low = acc0[:half] * shrink[:half]
        acc_high = acc0[half:] * shrink[half:]
    for at, (_, values, bias) in enumerate(pieces):
        p = jnp.exp2((scores[at] - (m - bias)) * scale)
        add = p[:, :128] + p[:, 128:]
        total = add if total is None else total + add
        w = p.astype(jnp.bfloat16)
        v = values()
        low = jnp.dot(w[:half], v[:, :128], preferred_element_type=jnp.float32)
        high = jnp.dot(w[half:], v[:, 128:], preferred_element_type=jnp.float32)
        acc_low = low if acc_low is None else acc_low + low
        acc_high = high if acc_high is None else acc_high + high
    return m, total, jnp.concatenate([acc_low, acc_high], axis=0)


def bias_of(keep_ref, block, count):
    safe = jnp.clip(block, 0, count - 1)
    ok = (block >= 0) & (block < count) & (keep_ref[safe] == 1)
    return jnp.where(ok, 0.0, MASKED)


def part_of(ref, start):
    return (
        lambda: ref[pl.ds(start, BLOCK)],
        lambda: ref[pl.ds(pl.multiple_of(start + BLOCK, BLOCK), BLOCK)],
    )


def attend_kernel(scale, heads, local, plan, stateful, finish, rotated, keep_ref, q_ref, *refs):
    arrays = 1 + max(max(array) if isinstance(array, tuple) else array for _, array, _, _ in plan)
    sources, refs = refs[:arrays], refs[arrays:]
    m0, l0, acc0 = None, None, None
    if stateful:
        m0, l0, acc0 = (ref[...] for ref in refs[:3])
        refs = refs[3:]
    if finish:
        w_ref, *outs, scores, near = refs
        out_refs = outs if rotated else [outs[0].at[at] for at in range(outs[0].shape[0])]
    else:
        m_ref, l_ref, acc_ref, scores, near = refs
    count = keep_ref.shape[0]
    rank = lax.axis_index("seq")
    block = rank * 2 + local
    pieces = []
    for what, array, start, number in plan:
        if what == "near":
            core_ref, halo_ref = sources[array[0]], sources[array[1]]
            mine = lax.rem(rank, 2) == local

            @pl.when(mine)
            def _():
                near[...] = halo_ref[...]

            @pl.when(jnp.logical_not(mine))
            def _():
                near[...] = core_ref[start : start + 2 * BLOCK]

            pieces.append((*part_of(near, 0), bias_of(keep_ref, block + number, count)))
        elif what == "self":
            pieces.append((*part_of(sources[array], start), 0.0))
        else:
            pieces.append((*part_of(sources[array], start), bias_of(keep_ref, block ^ number, count)))
    q = q_ref[local * BLOCK : (local + 1) * BLOCK]
    m, total, acc = fold(pieces, q, scores, scale, heads, m0, l0, acc0)
    if not finish:
        m_ref[...] = jnp.broadcast_to(m, m_ref.shape)
        l_ref[...] = total
        acc_ref[...] = acc
        return
    mixed = acc / jnp.sum(total, axis=1, keepdims=True)
    lane = lax.broadcasted_iota(jnp.int32, (BLOCK, 128), 1)
    joined = []
    for pair in range(2):
        first = mixed[2 * pair * BLOCK : (2 * pair + 1) * BLOCK]
        second = mixed[(2 * pair + 1) * BLOCK : (2 * pair + 2) * BLOCK]
        joined.append(jnp.where(lane < HD, first, second))
    attended = jnp.concatenate(joined, axis=1).astype(jnp.bfloat16)
    groups = len(out_refs)
    columns = out_refs[0].shape[1]
    for group, out_ref in enumerate(out_refs):
        start = group * columns
        if rotated:
            start = pl.multiple_of(lax.rem(lax.axis_index("head") + group, groups) * columns, columns)
        w = w_ref[:, pl.ds(start, columns)]
        out_ref[...] = jnp.dot(attended, w, preferred_element_type=jnp.float32).astype(out_ref.dtype)


def attend(name, block_keep, queries, local, sources, plan, state=None, w_out=None, rotated=False):
    width = queries.shape[1]
    heads = width // HD
    stacked = heads * BLOCK
    scale = 1.0 / math.sqrt(HD) * math.log2(math.e)
    vmem = pl.BlockSpec(memory_space=pltpu.VMEM)
    smem = pl.BlockSpec(memory_space=pltpu.SMEM)
    finish = w_out is not None
    if finish:
        groups = lax.axis_size("head")
        columns = w_out.shape[1] // groups
        if rotated:
            shape = [jax.ShapeDtypeStruct((BLOCK, columns), jnp.bfloat16)] * groups
            specs = [vmem] * groups
        else:
            shape = jax.ShapeDtypeStruct((groups, BLOCK, columns), jnp.bfloat16)
            specs = vmem
    else:
        shape = [jax.ShapeDtypeStruct((stacked, 128), jnp.float32)] * 3
        specs = [vmem] * 3
    given = [block_keep, queries, *sources, *(state or ()), *((w_out,) if finish else ())]
    return pl.pallas_call(
        lambda *refs: attend_kernel(scale, heads, local, plan, state is not None, finish, rotated, *refs),
        out_shape=shape,
        in_specs=[smem] + [vmem] * (len(given) - 1),
        out_specs=specs,
        scratch_shapes=[
            pltpu.VMEM((len(plan), stacked, BLOCK), jnp.float32),
            pltpu.VMEM((2 * BLOCK, width), jnp.bfloat16),
        ],
        compiler_params=pltpu.CompilerParams(vmem_limit_bytes=(len(plan) + 7) << 20),
        cost_estimate=pl.CostEstimate(
            flops=len(plan) * 4 * stacked * BLOCK * width * COST,
            transcendentals=len(plan) * stacked * BLOCK,
            bytes_accessed=len(plan) * 2 * BLOCK * width * 2,
        ),
        name=name,
    )(*given)


def per_device(queries, keys, values, block_keep, w_out):
    parts = [
        jnp.concatenate([keys[at : at + BLOCK], values[at : at + BLOCK]], axis=0) for at in (0, BLOCK)
    ]
    packed = jnp.concatenate(parts, axis=0)
    side = lax.rem(lax.axis_index("seq"), 2)
    edge = jnp.where(side == 1, parts[1], parts[0])
    core = flat_exchange(packed, "seq", 1)
    halo = halo_exchange(edge, "seq")
    y4a = flat_exchange(parts[0], "seq", 1 << 3)
    y2a = flat_exchange(parts[0], "seq", 1 << 2)
    y1 = flat_exchange(after(packed, halo), "seq", 1 << 1)
    x1 = flat_exchange(after(packed, halo), "seq", 1 << 4)
    x2 = flat_exchange(after(packed, halo), "seq", 1 << 5)
    z1 = flat_exchange(after(packed, y1), "seq", 1 << 6)
    y2b = flat_exchange(after(parts[1], y1), "seq", 1 << 2)
    y4b = flat_exchange(after(parts[1], y1), "seq", 1 << 3)

    state0 = attend(
        "early0",
        block_keep,
        queries,
        0,
        [packed, core, halo],
        [
            ("self", 0, 0, 0),
            ("xor", 0, 512, 1),
            ("xor", 1, 0, 2),
            ("near", (1, 2), 512, -1),
        ],
    )
    state1 = attend(
        "early1",
        block_keep,
        queries,
        1,
        [packed, core, halo],
        [
            ("self", 0, 512, 0),
            ("xor", 0, 0, 1),
            ("xor", 1, 512, 2),
            ("near", (1, 2), 0, 1),
        ],
    )
    first = attend(
        "late0",
        block_keep,
        after(queries, state1[0]),
        0,
        [z1, y1, x1, x2, y2a, y4a],
        [
            ("xor", 0, 0, 128),
            ("xor", 1, 0, 4),
            ("xor", 2, 0, 32),
            ("xor", 3, 0, 64),
            ("xor", 4, 0, 8),
            ("xor", 5, 0, 16),
        ],
        state=state0,
        w_out=w_out,
    )
    spread = [lax.all_to_all(first, "head", 0, 0, tiled=False)]
    shares = attend(
        "late1",
        block_keep,
        after(queries, first),
        1,
        [z1, y1, x1, x2, y2b, y4b],
        [
            ("xor", 0, 512, 128),
            ("xor", 1, 512, 4),
            ("xor", 2, 512, 32),
            ("xor", 3, 512, 64),
            ("xor", 4, 0, 8),
            ("xor", 5, 0, 16),
        ],
        state=state1,
        w_out=w_out,
    )
    spread.append(lax.all_to_all(after(shares, spread[0]), "head", 0, 0, tiled=False))
    outs = [jnp.sum(piece.astype(jnp.float32), axis=0).astype(jnp.bfloat16) for piece in spread]
    return jnp.concatenate(outs, axis=0)


def solution(mesh):
    placed = (P("seq", "head"), P("seq", "head"), P("seq", "head"), P(), P("head", None))
    return jax.shard_map(
        per_device, mesh=mesh, in_specs=placed, out_specs=P("seq", "head"), check_vma=False
    )
```

```python
import math

import jax
import jax.numpy as jnp
from jax import lax
from jax.experimental import pallas as pl
from jax.experimental.pallas import tpu as pltpu
from jax.sharding import PartitionSpec as P

HD = 64
BLOCK = 256
MASKED = -1e30
COST = 4


def flat_exchange(value, axis, mask):
    pairs = [(source, source ^ mask) for source in range(lax.axis_size(axis))]
    return lax.ppermute(value, axis, pairs)


def halo_exchange(value, axis):
    count = lax.axis_size(axis)
    pairs = []
    for source in range(count):
        target = source + 1 if source % 2 else source - 1
        if 0 <= target < count:
            pairs.append((source, target))
    return lax.ppermute(value, axis, pairs)


def after(value, *others):
    return lax.optimization_barrier((value, *others))[0]


def stacked_heads(q, heads):
    lane = lax.broadcasted_iota(jnp.int32, q.shape, 1)
    zero = jnp.zeros_like(q)
    return jnp.concatenate(
        [jnp.where((lane >= h * HD) & (lane < (h + 1) * HD), q, zero) for h in range(heads)], axis=0
    )


def fold(pieces, q, scores, scale, heads, m0, l0, acc0):
    qs = stacked_heads(q, heads)
    rows = qs.shape[0]
    half = rows // 2
    part = m0
    for at, (keys, _, bias) in enumerate(pieces):
        s = lax.dot_general(qs, keys(), (((1,), (1,)), ((), ())), preferred_element_type=jnp.float32)
        scores[at] = s
        top = jnp.maximum(s[:, :128], s[:, 128:]) + bias
        part = top if part is None else jnp.maximum(part, top)
    m = jnp.max(part, axis=1, keepdims=True)
    if l0 is None:
        total, acc_low, acc_high = None, None, None
    else:
        shrink = jnp.exp2((m0 - m) * scale)
        total = l0 * shrink
        acc_low = acc0[:half] * shrink[:half]
        acc_high = acc0[half:] * shrink[half:]
    for at, (_, values, bias) in enumerate(pieces):
        p = jnp.exp2((scores[at] - (m - bias)) * scale)
        add = p[:, :128] + p[:, 128:]
        total = add if total is None else total + add
        w = p.astype(jnp.bfloat16)
        v = values()
        low = jnp.dot(w[:half], v[:, :128], preferred_element_type=jnp.float32)
        high = jnp.dot(w[half:], v[:, 128:], preferred_element_type=jnp.float32)
        acc_low = low if acc_low is None else acc_low + low
        acc_high = high if acc_high is None else acc_high + high
    return m, total, jnp.concatenate([acc_low, acc_high], axis=0)


def bias_of(keep_ref, block, count):
    safe = jnp.clip(block, 0, count - 1)
    ok = (block >= 0) & (block < count) & (keep_ref[safe] == 1)
    return jnp.where(ok, 0.0, MASKED)


def part_of(ref, start):
    return (
        lambda: ref[pl.ds(start, BLOCK)],
        lambda: ref[pl.ds(pl.multiple_of(start + BLOCK, BLOCK), BLOCK)],
    )


def attend_kernel(scale, heads, local, plan, stateful, finish, rotated, keep_ref, q_ref, *refs):
    arrays = 1 + max(max(array) if isinstance(array, tuple) else array for _, array, _, _ in plan)
    sources, refs = refs[:arrays], refs[arrays:]
    m0, l0, acc0 = None, None, None
    if stateful:
        m0, l0, acc0 = (ref[...] for ref in refs[:3])
        refs = refs[3:]
    if finish:
        w_ref, *outs, scores, near = refs
        out_refs = outs if rotated else [outs[0].at[at] for at in range(outs[0].shape[0])]
    else:
        m_ref, l_ref, acc_ref, scores, near = refs
    count = keep_ref.shape[0]
    rank = lax.axis_index("seq")
    block = rank * 2 + local
    pieces = []
    for what, array, start, number in plan:
        if what == "near":
            core_ref, halo_ref = sources[array[0]], sources[array[1]]
            mine = lax.rem(rank, 2) == local

            @pl.when(mine)
            def _():
                near[...] = halo_ref[...]

            @pl.when(jnp.logical_not(mine))
            def _():
                near[...] = core_ref[start : start + 2 * BLOCK]

            pieces.append((*part_of(near, 0), bias_of(keep_ref, block + number, count)))
        elif what == "self":
            pieces.append((*part_of(sources[array], start), 0.0))
        else:
            pieces.append((*part_of(sources[array], start), bias_of(keep_ref, block ^ number, count)))
    q = q_ref[local * BLOCK : (local + 1) * BLOCK]
    m, total, acc = fold(pieces, q, scores, scale, heads, m0, l0, acc0)
    if not finish:
        m_ref[...] = jnp.broadcast_to(m, m_ref.shape)
        l_ref[...] = total
        acc_ref[...] = acc
        return
    mixed = acc / jnp.sum(total, axis=1, keepdims=True)
    lane = lax.broadcasted_iota(jnp.int32, (BLOCK, 128), 1)
    joined = []
    for pair in range(2):
        first = mixed[2 * pair * BLOCK : (2 * pair + 1) * BLOCK]
        second = mixed[(2 * pair + 1) * BLOCK : (2 * pair + 2) * BLOCK]
        joined.append(jnp.where(lane < HD, first, second))
    attended = jnp.concatenate(joined, axis=1).astype(jnp.bfloat16)
    groups = len(out_refs)
    columns = out_refs[0].shape[1]
    for group, out_ref in enumerate(out_refs):
        start = group * columns
        if rotated:
            start = pl.multiple_of(lax.rem(lax.axis_index("head") + group, groups) * columns, columns)
        w = w_ref[:, pl.ds(start, columns)]
        out_ref[...] = jnp.dot(attended, w, preferred_element_type=jnp.float32).astype(out_ref.dtype)


def attend(name, block_keep, queries, local, sources, plan, state=None, w_out=None, rotated=False):
    width = queries.shape[1]
    heads = width // HD
    stacked = heads * BLOCK
    scale = 1.0 / math.sqrt(HD) * math.log2(math.e)
    vmem = pl.BlockSpec(memory_space=pltpu.VMEM)
    smem = pl.BlockSpec(memory_space=pltpu.SMEM)
    finish = w_out is not None
    if finish:
        groups = lax.axis_size("head")
        columns = w_out.shape[1] // groups
        if rotated:
            shape = [jax.ShapeDtypeStruct((BLOCK, columns), jnp.bfloat16)] * groups
            specs = [vmem] * groups
        else:
            shape = jax.ShapeDtypeStruct((groups, BLOCK, columns), jnp.bfloat16)
            specs = vmem
    else:
        shape = [jax.ShapeDtypeStruct((stacked, 128), jnp.float32)] * 3
        specs = [vmem] * 3
    given = [block_keep, queries, *sources, *(state or ()), *((w_out,) if finish else ())]
    return pl.pallas_call(
        lambda *refs: attend_kernel(scale, heads, local, plan, state is not None, finish, rotated, *refs),
        out_shape=shape,
        in_specs=[smem] + [vmem] * (len(given) - 1),
        out_specs=specs,
        scratch_shapes=[
            pltpu.VMEM((len(plan), stacked, BLOCK), jnp.float32),
            pltpu.VMEM((2 * BLOCK, width), jnp.bfloat16),
        ],
        compiler_params=pltpu.CompilerParams(vmem_limit_bytes=(len(plan) + 7) << 20),
        cost_estimate=pl.CostEstimate(
            flops=len(plan) * 4 * stacked * BLOCK * width * COST,
            transcendentals=len(plan) * stacked * BLOCK,
            bytes_accessed=len(plan) * 2 * BLOCK * width * 2,
        ),
        name=name,
    )(*given)


def per_device(queries, keys, values, block_keep, w_out):
    parts = [
        jnp.concatenate([keys[at : at + BLOCK], values[at : at + BLOCK]], axis=0) for at in (0, BLOCK)
    ]
    packed = jnp.concatenate(parts, axis=0)
    side = lax.rem(lax.axis_index("seq"), 2)
    edge = jnp.where(side == 1, parts[1], parts[0])
    core = flat_exchange(packed, "seq", 1)
    halo = halo_exchange(edge, "seq")
    y4a = flat_exchange(parts[0], "seq", 1 << 3)
    y2a = flat_exchange(parts[0], "seq", 1 << 2)
    y1 = flat_exchange(packed, "seq", 1 << 1)
    x1 = flat_exchange(after(packed, core), "seq", 1 << 4)
    x2 = flat_exchange(after(packed, core), "seq", 1 << 5)
    z1 = flat_exchange(after(packed, y1), "seq", 1 << 6)
    y2b = flat_exchange(after(parts[1], x1), "seq", 1 << 2)
    y4b = flat_exchange(after(parts[1], x1), "seq", 1 << 3)

    state0 = attend(
        "early0",
        block_keep,
        queries,
        0,
        [packed, core, halo],
        [
            ("self", 0, 0, 0),
            ("xor", 0, 512, 1),
            ("xor", 1, 0, 2),
            ("near", (1, 2), 512, -1),
        ],
    )
    state1 = attend(
        "early1",
        block_keep,
        queries,
        1,
        [packed, core, halo],
        [
            ("self", 0, 512, 0),
            ("xor", 0, 0, 1),
            ("xor", 1, 512, 2),
            ("near", (1, 2), 0, 1),
        ],
    )
    mine, *pieces = attend(
        "late0",
        block_keep,
        after(queries, state1[0]),
        0,
        [z1, y1, x1, x2, y2a, y4a],
        [
            ("xor", 0, 0, 128),
            ("xor", 1, 0, 4),
            ("xor", 2, 0, 32),
            ("xor", 3, 0, 64),
            ("xor", 4, 0, 8),
            ("xor", 5, 0, 16),
        ],
        state=state0,
        w_out=w_out,
        rotated=True,
    )
    groups = 1 + len(pieces)
    moved = [
        lax.ppermute(piece, "head", [(h, (h + hop + 1) % groups) for h in range(groups)])
        for hop, piece in enumerate(pieces)
    ]
    shares = attend(
        "late1",
        block_keep,
        after(queries, mine),
        1,
        [z1, y1, x1, x2, y2b, y4b],
        [
            ("xor", 0, 512, 128),
            ("xor", 1, 512, 4),
            ("xor", 2, 512, 32),
            ("xor", 3, 512, 64),
            ("xor", 4, 0, 8),
            ("xor", 5, 0, 16),
        ],
        state=state1,
        w_out=w_out,
    )
    spread = lax.all_to_all(after(shares, *moved), "head", 0, 0, tiled=False)
    total = mine.astype(jnp.float32)
    for piece in moved:
        total = total + piece.astype(jnp.float32)
    outs = [total, jnp.sum(spread.astype(jnp.float32), axis=0)]
    return jnp.concatenate([out.astype(jnp.bfloat16) for out in outs], axis=0)


def solution(mesh):
    placed = (P("seq", "head"), P("seq", "head"), P("seq", "head"), P(), P("head", None))
    return jax.shard_map(
        per_device, mesh=mesh, in_specs=placed, out_specs=P("seq", "head"), check_vma=False
    )
```
